32 devices in a mesh: tile: 8 (over z, y), rad: 4 (over x, core).
Axes of the slice: x: 2, y: 2, z: 4, core: 2. Of those that a mesh axis runs over, the one named last changes fastest.
Arguments:
- fields: float32 [8, 96, 64, 256], P(None, 'rad', 'tile'), may hold values from -6 to 6
- opacity: float32 [96, 64, 256], P('rad', 'tile'), may hold values from 0.0026041667 to 0.041666668
- donor_row: int32 [2048], P('tile'), may hold values from 0 to 4
- donor_column: int32 [2048], P('tile'), may hold values from 0 to 252
- target_tile: int32 [2048, 1], P('tile'), may hold values from 0 to 7; in each aligned block of 256 rows (0 to 255, 256 to 511, ...) at most 64 rows name the same one
- target_cell: int32 [2048], P('tile'), may hold values from 0 to 2047
- lagrange: float32 [16, 2048], P(None, 'tile'), may hold values from -0.2 to 0.5
Outputs:
- updated: float32 [8, 96, 64, 256], P(None, 'rad', 'tile')
The draws below stay inside these ranges and needn't reach their ends.
Inputs may be any that keep to these rules, and one draw needn't show every extreme that they name: `target_tile`: within the 256 donor points of one tile no target tile appears more than 64 times, and some target tile appears exactly 64 times.
All inputs are finite; a program needn't handle non-finite values.
Results may differ from the reference program's by a relative error of at most 0.00005.
Values sent between devices are 32-bit elements; how exact they have to be, the bound alone decides.
A program may use at most 64 MiB of HBM per device.

```python
import math
import jax
import jax.numpy as jnp
import numpy as np
from jax import lax

F = 8
ROWS = 8
COLS = 256
G_DEV = 256
CAP = 64
LEVELS = 96
NROWS = 64
TASKS = 2048
N_TILE = 8


def touch_ends(values, stream_key, least, largest):
    shape = values.shape
    spot = [jax.random.randint(jax.random.fold_in(stream_key, axis), (), 0, shape[axis]) for axis in range(len(shape))]
    values = values.at[tuple(spot)].set(least)
    longest = shape.index(max(shape))
    spot[longest] = (spot[longest] + 1) % shape[longest]
    return values.at[tuple(spot)].set(largest)


def levels(stream_key, shape, shards, least, largest):
    def one(axis_at, blocks):
        heights = jax.random.uniform(jax.random.fold_in(jax.random.fold_in(stream_key, 6), axis_at), (blocks,), jnp.float32, least / len(shards), largest / len(shards))
        return jnp.repeat(jnp.exp(heights), shape[axis_at] // blocks).reshape((-1,) + (1,) * (len(shape) - axis_at - 1))

    level = one(*shards[0])
    for cut in shards[1:]:
        level = level * one(*cut)
    return level


def shared_out(rng, own, number, rows, amount, top, most, skew):
    sequence = jax.random.permutation(rng, amount)
    crowded, common = shares(amount, rows * top, most, skew, True), shares(amount, rows * top, most, skew, False)
    places = jnp.arange(amount)

    def named(sizes, turn):
        used = int((sizes > 0).sum())
        fixed = max(1, used // 4)
        moved = fixed + (places - fixed + turn * (used - fixed)) % max(1, amount - fixed)
        return jnp.zeros((amount,), jnp.int32).at[sequence[jnp.where(places < fixed, places, moved)]].set(jnp.asarray(sizes, jnp.int32))

    sizes = jnp.where(number % 4 == 0, named(crowded, number // 4), named(common, number - number // 4 - 1))
    mixed = jax.random.permutation(jax.random.fold_in(own, 3), amount)
    donor, receiver = mixed[0:amount // 2 * 2:2], mixed[1:amount // 2 * 2:2]
    room = jnp.minimum(sizes[donor] - 1, most - sizes[receiver]) // 2
    room = jnp.where((donor == sequence[0]) | (receiver == sequence[0]) | (sizes[receiver] == 0), 0, jnp.maximum(room, 0))
    moved = jax.random.randint(jax.random.fold_in(own, 4), (amount // 2,), 0, 1 << 20) % (room + 1)
    sizes = sizes.at[donor].add(-moved).at[receiver].add(moved)
    items = jnp.searchsorted(jnp.cumsum(sizes), jnp.arange(rows * top), side="right").astype(jnp.int32)
    listing = items.reshape(top, rows).T
    listing = listing[jax.random.permutation(jax.random.fold_in(own, 1), rows)]
    turn = jax.random.randint(jax.random.fold_in(own, 2), (rows, 1), 0, top)
    return jnp.take_along_axis(listing, (jnp.arange(top)[None, :] + turn) % top, axis=1)


def shares(number_of, total, reach, skew, full):
    portions = [(1 << 20) // math.isqrt(rank ** skew) + 1 for rank in range(1, number_of + 1)]
    largest = reach if full else min(reach, max(-(-total // number_of), total * portions[0] // sum(portions)))
    least = 1 if total - largest >= number_of - 1 else 0
    given, surplus = [largest] + [least] * (number_of - 1), total - largest - least * (number_of - 1)
    while surplus > 0:
        candidates = [i for i in range(1, number_of) if given[i] < largest] or [i for i in range(1, number_of) if given[i] < reach]
        whole, budget = sum([portions[i] for i in candidates]), surplus
        for i in candidates:
            addition = min(reach - given[i], max(1, budget * portions[i] // whole), surplus)
            given[i] = given[i] + addition
            surplus = surplus - addition
    return np.array(given)


def noise(key, shape, deviation, most, pieces=(), held_as=jnp.bfloat16):
    entries = jax.random.normal(key, shape, jnp.float32) * deviation
    if len(pieces) > 0:
        entries = levels(key, shape, pieces, -0.22, 0.18) * entries
    return jnp.clip(entries, min=-most, max=most).astype(held_as)


def setup_inputs(seed: int = 0) -> dict:
    streams_of = jax.random.split(jax.random.key(seed), 8)
    fields = noise(streams_of[0], (F, LEVELS, NROWS, COLS), 1.0, 6.0, ((1, 4), (2, 8)), jnp.float32)
    opacity = jnp.clip(jnp.exp(math.log(0.041666668) - 2.7725887 * jax.random.uniform(streams_of[1], (LEVELS, NROWS, COLS), jnp.float32) ** levels(streams_of[1], (LEVELS, NROWS, COLS), ((0, 4), (1, 8)), -0.2, 0.2)), 0.0026041667, 0.041666668)
    donor_row = touch_ends(jax.random.randint(streams_of[2], (TASKS,), 0, ROWS - 3), jax.random.fold_in(streams_of[2], 1), 0, (ROWS - 3) - 1).astype(jnp.int32)
    donor_column = touch_ends(jax.random.randint(streams_of[3], (TASKS,), 0, COLS - 3), jax.random.fold_in(streams_of[3], 1), 0, (COLS - 3) - 1).astype(jnp.int32)
    target_tile_keys = jax.random.split(jax.random.fold_in(streams_of[4], 1), TASKS // G_DEV)
    target_tile_turns = jax.random.permutation(jax.random.fold_in(streams_of[4], 3), TASKS // G_DEV)
    target_tile = jax.vmap(lambda own, number: shared_out(jax.random.fold_in(streams_of[4], 2), own, number, G_DEV, N_TILE, 1, CAP, 2))(target_tile_keys, target_tile_turns).reshape((TASKS, 1))
    target_cell = touch_ends(jax.random.randint(streams_of[5], (TASKS,), 0, ROWS * COLS), jax.random.fold_in(streams_of[5], 1), 0, (ROWS * COLS) - 1).astype(jnp.int32)
    lagrange = jnp.clip(-0.2 + 0.7 * jax.random.uniform(streams_of[6], (16, TASKS), jnp.float32) ** levels(streams_of[6], (16, TASKS), ((1, 8),), -0.2, 0.2), -0.2, 0.5)
    return dict(fields=fields, opacity=opacity, donor_row=donor_row, donor_column=donor_column, target_tile=target_tile, target_cell=target_cell, lagrange=lagrange)


FIRST_WEIGHTS = (-1.0 / 60.0, 9.0 / 60.0, -45.0 / 60.0, 0.0, 45.0 / 60.0, -9.0 / 60.0, 1.0 / 60.0)
SECOND_WEIGHTS = (2.0 / 180.0, -27.0 / 180.0, 270.0 / 180.0, -490.0 / 180.0, 270.0 / 180.0, -27.0 / 180.0, 2.0 / 180.0)
VISCOSITY = 0.1
COUPLING = 1.0
COOL_RATE = 2.0
TIME_STEP = 0.2


def stencil(padded, dimension, length, weights):
    running = None
    for offset, weight in enumerate(weights):
        if weight == 0.0:
            continue
        shifted = weight * lax.slice_in_dim(padded, offset, offset + length, axis=dimension)
        running = shifted if running is None else running + shifted
    return running


def reference(fields, opacity, donor_row, donor_column, target_tile, target_cell, lagrange):
    half_rows = NROWS // 2
    quarter_rows = NROWS // 4
    radial_speed = fields[1]
    row_speed = fields[2]
    column_speed = fields[3]

    def row_terms(single, weights):
        rolled = jnp.roll(single, quarter_rows, axis=1)
        panels = rolled.reshape(LEVELS, 2, half_rows, COLS)
        panel_pad = jnp.pad(panels, ((0, 0), (0, 0), (3, 3), (0, 0)))
        result = stencil(panel_pad, 2, half_rows, weights).reshape(LEVELS, NROWS, COLS)
        return jnp.roll(result, -quarter_rows, axis=1)

    def tendency_of(single):
        radial_pad = jnp.pad(single, ((3, 3), (0, 0), (0, 0)))
        column_pad = jnp.pad(single, ((0, 0), (0, 0), (3, 3)))
        advect = radial_speed * stencil(radial_pad, 0, LEVELS, FIRST_WEIGHTS)
        advect = advect + row_speed * row_terms(single, FIRST_WEIGHTS)
        advect = advect + column_speed * stencil(column_pad, 2, COLS, FIRST_WEIGHTS)
        diffuse = stencil(radial_pad, 0, LEVELS, SECOND_WEIGHTS)
        diffuse = diffuse + row_terms(single, SECOND_WEIGHTS)
        diffuse = diffuse + stencil(column_pad, 2, COLS, SECOND_WEIGHTS)
        return VISCOSITY * diffuse - advect

    base = lax.map(tendency_of, fields)

    flattened = fields.reshape(F, LEVELS, NROWS * COLS)
    sender = jnp.arange(TASKS, dtype=jnp.int32) // G_DEV
    base_row = sender * ROWS + donor_row
    stencil_pos = jnp.arange(16, dtype=jnp.int32)
    indices = (base_row[None, :] + (stencil_pos // 4)[:, None]) * COLS + donor_column[None, :] + (stencil_pos % 4)[:, None]
    indices = indices.reshape(16, N_TILE, G_DEV).transpose(1, 0, 2)
    weights_all = lagrange.reshape(16, N_TILE, G_DEV).transpose(1, 0, 2)

    def interpolate(pair):
        block_index, block_weight = pair
        picked = flattened[:, :, block_index]
        return jnp.sum(picked * block_weight[None, None], axis=2)

    values = lax.map(interpolate, (indices, weights_all))
    values = values.transpose(1, 2, 0, 3).reshape(F, LEVELS, TASKS)
    destination = target_tile[:, 0] * (ROWS * COLS) + target_cell
    boundary = jnp.zeros((F, LEVELS, NROWS * COLS), jnp.float32).at[:, :, destination].add(values)
    counts = jnp.zeros((NROWS * COLS,), jnp.float32).at[destination].add(1.0)
    penalty = COUPLING * (boundary - counts * flattened)
    tendency = base + penalty.reshape(F, LEVELS, NROWS, COLS)

    optical_depth = jnp.cumsum(opacity, axis=0) - 0.5 * opacity
    cooling = -COOL_RATE * jnp.exp(-optical_depth) * fields[7]
    tendency = tendency.at[7].add(cooling)
    return fields + TIME_STEP * tendency
```

```python
import functools

import jax
import jax.numpy as jnp
from jax import lax
from jax.experimental import pallas as pl
from jax.experimental.pallas import tpu as pltpu
from jax.sharding import PartitionSpec as P

VISCOSITY = 0.1
COUPLING = 1.0
COOL_RATE = 2.0
TIME_STEP = 0.2
MESH = pl.DeviceIdType.MESH
LANES = 128
VMEM_LIMIT = 32 << 20
STEP = 4
EARLY = 2
NT = (((1,), (1,)), ((), ()))


def in_hbm(x):
    return pltpu.with_memory_space_constraint(x, pltpu.HBM)


def dot(a, b):
    return jnp.dot(a, b, preferred_element_type=jnp.float32)


def split(x):
    high = x.astype(jnp.bfloat16)
    low = (x - high.astype(jnp.float32)).astype(jnp.bfloat16)
    return high, low


def pair_terms(u, ups, downs):
    s1, s2, s3 = [a + b for a, b in zip(ups, downs)]
    d1, d2, d3 = [a - b for a, b in zip(ups, downs)]
    first = (45.0 / 60.0) * d1 - (9.0 / 60.0) * d2 + (1.0 / 60.0) * d3
    second = (
        (270.0 / 180.0) * s1 - (27.0 / 180.0) * s2 + (2.0 / 180.0) * s3 - (490.0 / 180.0) * u
    )
    return first, second


def kernel(
    n_tile, n_rad, inner, cap,
    f4, f2, opacity, drow, dcol, ttile, tcell, lagrange,
    acc,
    x2, ext, psend, precv, relay, ghost, hits, chunks, inc, xall, opsum, oprecv,
    x2_sem, in_sem, lvl_send, lvl_recv, row_send, row_recv, hop_recv, fwd_send, op_send, op_recv,
    a2a_send, a2a_recv,
):
    F, L, R, C = acc.shape
    V = F * L
    T = drow.shape[1]
    pack = LANES // cap
    VP = V // pack
    tile = lax.axis_index("tile")
    rad = lax.axis_index("rad")
    quarter = n_tile // 4

    halves = C // LANES
    load_x2 = [
        pltpu.make_async_copy(f2.at[:, pl.ds(h * LANES, LANES)], x2.at[h], x2_sem.at[h])
        for h in range(halves)
    ]
    load_ext = pltpu.make_async_copy(f4, ext.at[:, pl.ds(3, L)], in_sem)
    for copy in load_x2:
        copy.start()
    load_ext.start()

    barrier = pltpu.get_barrier_semaphore()
    for d in range(1, n_tile):
        pl.semaphore_signal(
            barrier, inc=1, device_id=(lax.rem(tile + d, n_tile), rad), device_id_type=MESH
        )
    for d in range(1, n_rad):
        pl.semaphore_signal(
            barrier, inc=1, device_id=(tile, lax.rem(rad + d, n_rad)), device_id_type=MESH
        )

    opsum[...] = jnp.sum(opacity[...], axis=0)
    for copy in load_x2:
        copy.wait()

    nxt = lax.rem(tile + 1, n_tile)
    prv = lax.rem(tile + n_tile - 1, n_tile)
    has_next = jnp.logical_and(tile != quarter - 1, tile != 3 * quarter - 1)
    has_prev = jnp.logical_and(tile != quarter, tile != 3 * quarter)
    has_above = rad != n_rad - 1
    has_below = rad != 0

    for f in range(F):
        for j in range(3):
            for h in range(halves):
                side = pl.ds(h * LANES, LANES)
                psend[f, 0, j, :, side] = x2[h, pl.ds(f * L * R + R - 3 + j, L, stride=R), :]
                psend[f, 1, j, :, side] = x2[h, pl.ds(f * L * R + j, L, stride=R), :]

    pl.semaphore_wait(barrier, n_tile - 1 + n_rad - 1)

    lvl_up = pltpu.make_async_remote_copy(
        src_ref=f4.at[:, pl.ds(L - 3, 3)], dst_ref=ext.at[:, pl.ds(0, 3)],
        send_sem=lvl_send.at[0], recv_sem=lvl_recv.at[0],
        device_id=(tile, lax.rem(rad + 1, n_rad)), device_id_type=MESH,
    )
    lvl_down = pltpu.make_async_remote_copy(
        src_ref=f4.at[:, pl.ds(0, 3)], dst_ref=ext.at[:, pl.ds(L + 3, 3)],
        send_sem=lvl_send.at[1], recv_sem=lvl_recv.at[1],
        device_id=(tile, lax.rem(rad + n_rad - 1, n_rad)), device_id_type=MESH,
    )

    @pl.when(has_above)
    def _():
        lvl_up.start()

    @pl.when(has_below)
    def _():
        lvl_down.start()

    op_copies = []
    for d in range(1, n_rad):
        copy = pltpu.make_async_remote_copy(
            src_ref=opsum, dst_ref=oprecv.at[d - 1],
            send_sem=op_send.at[d - 1], recv_sem=op_recv.at[d - 1],
            device_id=(tile, lax.rem(rad + d, n_rad)), device_id_type=MESH,
        )
        copy.start()
        op_copies.append(copy)

    half = F // 2
    relays = inner < n_tile
    place = lax.rem(tile, inner)
    crosses = (place == inner - 1, place == 0)
    partner = (nxt, prv)
    via = (tile - (inner - 1), tile + (inner - 1))
    sends = (has_next, has_prev)
    origin = (lax.rem(tile + inner - 1, n_tile), lax.rem(tile + n_tile - inner + 1, n_tile))
    forwards = (
        jnp.logical_and(
            crosses[1],
            jnp.logical_and(origin[0] != quarter - 1, origin[0] != 3 * quarter - 1),
        ),
        jnp.logical_and(
            crosses[0], jnp.logical_and(origin[1] != quarter, origin[1] != 3 * quarter)
        ),
    )
    goal = (lax.rem(origin[0] + 1, n_tile), lax.rem(origin[1] + n_tile - 1, n_tile))

    def row_copy(f, way):
        return pltpu.make_async_remote_copy(
            src_ref=psend.at[f, way], dst_ref=precv.at[f, way],
            send_sem=row_send.at[f, way], recv_sem=row_recv.at[f, way],
            device_id=(partner[way], rad), device_id_type=MESH,
        )

    def hop_copy(f, way):
        return pltpu.make_async_remote_copy(
            src_ref=psend.at[f, way], dst_ref=relay.at[f - half, way],
            send_sem=row_send.at[f, way], recv_sem=hop_recv.at[f - half, way],
            device_id=(via[way], rad), device_id_type=MESH,
        )

    def forward_copy(f, way):
        return pltpu.make_async_remote_copy(
            src_ref=relay.at[f - half, way], dst_ref=precv.at[f, way],
            send_sem=fwd_send.at[f - half, way], recv_sem=row_recv.at[f, way],
            device_id=(goal[way], rad), device_id_type=MESH,
        )

    def hops(f):
        return relays and f >= half

    def start_rows(fields, hopping):
        for f in fields:
            for way in range(2):
                if not hops(f):
                    if not hopping:
                        @pl.when(sends[way])
                        def _():
                            row_copy(f, way).start()
                elif hopping:
                    @pl.when(jnp.logical_and(sends[way], crosses[way]))
                    def _():
                        hop_copy(f, way).start()
                else:
                    @pl.when(jnp.logical_and(sends[way], jnp.logical_not(crosses[way])))
                    def _():
                        row_copy(f, way).start()

    start_rows(range(half, F), True)
    start_rows(range(EARLY), False)

    values = jnp.zeros((V, T), jnp.float32)
    diff = lax.broadcasted_iota(jnp.int32, (C, T), 0) - dcol[...]
    rows = drow[...]
    for r in range(R):
        weights = []
        for b in range(4):
            w = jnp.zeros((1, T), jnp.float32)
            for a in range(4):
                w = jnp.where(rows + a == r, lagrange[4 * a + b : 4 * a + b + 1, :], w)
            weights.append(w)
        g = jnp.where(diff == 0, weights[0], 0.0)
        for b in range(1, 4):
            g = jnp.where(diff == b, weights[b], g)
        gh, gl = split(g)
        xh, xl = split(
            jnp.concatenate([x2[h, pl.ds(r, V, stride=R), :] for h in range(halves)], axis=1)
        )
        values = values + (dot(xh, gh) + (dot(xl, gh) + dot(xh, gl)))

    target = ttile[...]
    kinds = max(16, n_tile)
    hot = (lax.broadcasted_iota(jnp.int32, (kinds, T), 0) == target).astype(jnp.float32)
    before = (
        lax.broadcasted_iota(jnp.int32, (T, T), 0) < lax.broadcasted_iota(jnp.int32, (T, T), 1)
    ).astype(jnp.float32)
    earlier = dot(hot.astype(jnp.bfloat16), before.astype(jnp.bfloat16))
    rank = jnp.sum(earlier * hot, axis=0, keepdims=True)
    key = target * cap + rank.astype(jnp.int32)
    lane_slot = lax.rem(lax.broadcasted_iota(jnp.int32, (LANES, T), 0), cap)
    vh, vl = split(values)
    label = tcell[...]
    side = lax.broadcasted_iota(jnp.int32, (16, T), 0)
    label = jnp.where(
        side == 0, label // C + 1, jnp.where(side == 1, lax.rem(label, C), 0)
    ).astype(jnp.float32).astype(jnp.bfloat16)
    stacked = jnp.concatenate([vh, vl, label], axis=0)
    lane_group = lax.broadcasted_iota(jnp.int32, (VP, LANES), 1) // cap

    def chunk(d):
        first = lax.rem(tile + d, n_tile) * cap
        chosen = (key == lane_slot + first).astype(jnp.float32).astype(jnp.bfloat16)
        moved = lax.dot_general(stacked, chosen, NT, preferred_element_type=jnp.float32)
        full = moved[:V] + moved[V : 2 * V]
        picked = full[:VP]
        for g in range(1, pack):
            picked = jnp.where(lane_group == g, full[g * VP : (g + 1) * VP], picked)
        return picked, moved[2 * V : 2 * V + 8]

    picked, marks = chunk(0)
    inc[0, pl.ds(0, VP)] = picked
    inc[0, pl.ds(VP, 8)] = marks

    def a2a_copy(d):
        return pltpu.make_async_remote_copy(
            src_ref=chunks.at[d], dst_ref=inc.at[d],
            send_sem=a2a_send.at[d], recv_sem=a2a_recv.at[d],
            device_id=(lax.rem(tile + d, n_tile), rad), device_id_type=MESH,
        )

    def send_chunk(d):
        picked, marks = chunk(d)
        chunks[d, pl.ds(0, VP)] = picked
        chunks[d, pl.ds(VP, 8)] = marks
        a2a_copy(d).start()

    if n_tile <= 8:
        for d in range(1, n_tile):
            send_chunk(d)
    else:
        lax.fori_loop(1, n_tile, lambda d, c: (send_chunk(d), c)[1], 0)

    start_rows(range(EARLY, F), False)
    if relays:
        for f in range(half, F):
            for way in range(2):
                @pl.when(forwards[way])
                def _():
                    hop_copy(f, way).wait_recv()
                    forward_copy(f, way).start()

    load_ext.wait()
    zeros3 = jnp.zeros((F, 3, R, C), jnp.float32)

    @pl.when(has_below)
    def _():
        lvl_up.wait_recv()

    @pl.when(jnp.logical_not(has_below))
    def _():
        ext[:, pl.ds(0, 3)] = zeros3

    @pl.when(has_above)
    def _():
        lvl_down.wait_recv()

    @pl.when(jnp.logical_not(has_above))
    def _():
        ext[:, pl.ds(L + 3, 3)] = zeros3

    column = lax.broadcasted_iota(jnp.int32, (STEP, R, C), 2)

    def local_part(i, carry):
        f = i // (L // STEP)
        l = lax.rem(i, L // STEP) * STEP
        u = ext[f, pl.ds(l + 3, STEP)]
        speed1 = ext[1, pl.ds(l + 3, STEP)]
        speed3 = ext[3, pl.ds(l + 3, STEP)]
        ups = [ext[f, pl.ds(l + 3 + k, STEP)] for k in (1, 2, 3)]
        downs = [ext[f, pl.ds(l + 3 - k, STEP)] for k in (1, 2, 3)]
        first, second = pair_terms(u, ups, downs)
        total = VISCOSITY * second - speed1 * first
        ups = [jnp.where(column < C - k, pltpu.roll(u, C - k, 2), 0.0) for k in (1, 2, 3)]
        downs = [jnp.where(column >= k, pltpu.roll(u, k, 2), 0.0) for k in (1, 2, 3)]
        first, second = pair_terms(u, ups, downs)
        acc[f, pl.ds(l, STEP)] = total + (VISCOSITY * second - speed3 * first)
        return carry

    lax.fori_loop(0, F * (L // STEP), local_part, 0)

    above = jnp.zeros((R, C), jnp.float32)
    for d in range(1, n_rad):
        op_copies[d - 1].wait_recv()
        above = above + jnp.where(rad >= d, oprecv[d - 1], 0.0)

    def cool(l, so_far):
        mine = opacity[l]
        depth = so_far + 0.5 * mine
        acc[7, l] = acc[7, l] - COOL_RATE * jnp.exp(-depth) * ext[7, l + 3]
        return so_far + mine

    lax.fori_loop(0, L, cool, above)

    for d in range(1, n_tile):
        a2a_copy(d).wait_recv()
    group_of = lax.broadcasted_iota(jnp.int32, (1, LANES), 1) // cap
    row_marks = []
    column_marks = []
    for d0 in range(0, n_tile, pack):
        lanes = pl.ds(d0 // pack * LANES, LANES)
        parts = [inc[d0 + j] for j in range(pack)]
        for g in range(pack):
            joined = None
            for j in range(pack):
                part = parts[j][:VP]
                turn = ((j - g) * cap) % LANES
                if turn:
                    part = pltpu.roll(part, turn, 1)
                joined = part if joined is None else jnp.where(lane_group == j, part, joined)
            high, low = split(joined)
            xall[pl.ds(g * VP, VP), lanes] = high
            xall[pl.ds(V + g * VP, VP), lanes] = low
        xall[pl.ds(2 * V, 16), lanes] = jnp.ones((16, LANES), jnp.bfloat16)
        row_mark = parts[0][VP : VP + 1]
        column_mark = parts[0][VP + 1 : VP + 2]
        for j in range(1, pack):
            row_mark = jnp.where(group_of == j, parts[j][VP : VP + 1], row_mark)
            column_mark = jnp.where(group_of == j, parts[j][VP + 1 : VP + 2], column_mark)
        row_marks.append(row_mark)
        column_marks.append(column_mark)
    row_mark = jnp.concatenate(row_marks, axis=1).astype(jnp.int32)
    column_mark = jnp.concatenate(column_marks, axis=1).astype(jnp.int32)
    slots = n_tile * cap
    cell_column = lax.broadcasted_iota(jnp.int32, (C, slots), 0)
    everything = xall[...]
    for r in range(R):
        wanted = jnp.where(row_mark == r + 1, column_mark, -1)
        place = (cell_column == wanted).astype(jnp.float32).astype(jnp.bfloat16)
        got = lax.dot_general(everything, place, NT, preferred_element_type=jnp.float32)
        total = got[:V] + got[V : 2 * V]
        for h in range(halves):
            ghost[h, pl.ds(r, V, stride=R), :] = total[:, h * LANES : (h + 1) * LANES]
        hits[pl.ds(r, 1), :] = got[2 * V : 2 * V + 1]

    row = lax.broadcasted_iota(jnp.int32, (STEP, R, C), 1)
    planes = x2

    for f in range(F):
        @pl.when(has_prev)
        def _():
            row_copy(f, 0).wait_recv()

        @pl.when(jnp.logical_not(has_prev))
        def _():
            precv[f, 0] = jnp.zeros((3, L, C), jnp.float32)

        @pl.when(has_next)
        def _():
            row_copy(f, 1).wait_recv()

        @pl.when(jnp.logical_not(has_next))
        def _():
            precv[f, 1] = jnp.zeros((3, L, C), jnp.float32)

        for j in range(3):
            for h in range(halves):
                side = pl.ds(h * LANES, LANES)
                planes[h, pl.ds(f * L * R + R - 3 + j, L, stride=R), :] = precv[f, 0, j, :, side]
                planes[h, pl.ds(f * L * R + j, L, stride=R), :] = precv[f, 1, j, :, side]

        def row_part(i, carry):
            l = i * STEP
            u = ext[f, pl.ds(l + 3, STEP)]
            speed2 = ext[2, pl.ds(l + 3, STEP)]
            at = pl.ds(pl.multiple_of((f * L + l) * R, STEP * R), STEP * R)
            edge = jnp.concatenate(
                [planes[h, at, :].reshape(STEP, R, LANES) for h in range(halves)], axis=2
            )
            arrived = jnp.concatenate(
                [ghost[h, at, :].reshape(STEP, R, LANES) for h in range(halves)], axis=2
            )
            ups = [pltpu.roll(jnp.where(row < k, edge, u), R - k, 1) for k in (1, 2, 3)]
            downs = [pltpu.roll(jnp.where(row >= R - k, edge, u), k, 1) for k in (1, 2, 3)]
            first, second = pair_terms(u, ups, downs)
            total = acc[f, pl.ds(l, STEP)] + (VISCOSITY * second - speed2 * first)
            total = total + COUPLING * (arrived - hits[...] * u)
            acc[f, pl.ds(l, STEP)] = u + TIME_STEP * total
            return carry

        lax.fori_loop(0, L // STEP, row_part, 0)

    @pl.when(has_above)
    def _():
        lvl_up.wait_send()

    @pl.when(has_below)
    def _():
        lvl_down.wait_send()

    for copy in op_copies:
        copy.wait_send()
    for d in range(1, n_tile):
        a2a_copy(d).wait_send()
    for f in range(F):
        for way in range(2):
            @pl.when(sends[way])
            def _():
                row_copy(f, way).wait_send()

            if hops(f):
                @pl.when(forwards[way])
                def _():
                    forward_copy(f, way).wait_send()


def shards(n_tile, n_rad, inner, fields, opacity, donor_row, donor_column, target_tile, target_cell, lagrange):
    F, L, R, C = fields.shape
    V = F * L
    T = donor_row.shape[0]
    cap = max(16, 2 * T // n_tile)
    pack = LANES // cap
    VP = V // pack
    hbm = pl.BlockSpec(memory_space=pltpu.HBM)
    vmem = pl.BlockSpec(memory_space=pltpu.VMEM)
    dma = pltpu.SemaphoreType.DMA
    f32 = jnp.float32
    return pl.pallas_call(
        functools.partial(kernel, n_tile, n_rad, inner, cap),
        out_shape=pltpu.VMEM(fields.shape, f32),
        in_specs=[hbm, hbm] + [vmem] * 6,
        out_specs=vmem,
        scratch_shapes=[
            pltpu.VMEM((C // LANES, V * R, LANES), f32),
            pltpu.VMEM((F, L + 6, R, C), f32),
            pltpu.VMEM((F, 2, 3, L, C), f32),
            pltpu.VMEM((F, 2, 3, L, C), f32),
            pltpu.VMEM((F - F // 2, 2, 3, L, C), f32),
            pltpu.VMEM((C // LANES, V * R, LANES), f32),
            pltpu.VMEM((R, C), f32),
            pltpu.VMEM((n_tile, VP + 8, LANES), f32),
            pltpu.VMEM((n_tile, VP + 8, LANES), f32),
            pltpu.VMEM((2 * V + 16, n_tile * cap), jnp.bfloat16),
            pltpu.VMEM((R, C), f32),
            pltpu.VMEM((n_rad - 1, R, C), f32),
            dma((C // LANES,)),
            dma(()),
            dma((2,)),
            dma((2,)),
            dma((F, 2)),
            dma((F, 2)),
            dma((F - F // 2, 2)),
            dma((F - F // 2, 2)),
            dma((n_rad - 1,)),
            dma((n_rad - 1,)),
            dma((n_tile,)),
            dma((n_tile,)),
        ],
        compiler_params=pltpu.CompilerParams(
            collective_id=0, has_side_effects=True, vmem_limit_bytes=VMEM_LIMIT
        ),
    )(
        in_hbm(fields),
        in_hbm(fields.reshape(V * R, C)),
        in_hbm(opacity),
        in_hbm(donor_row.reshape(1, T)),
        in_hbm(donor_column.reshape(1, T)),
        in_hbm(target_tile.reshape(1, T)),
        in_hbm(target_cell.reshape(1, T)),
        in_hbm(lagrange),
    )


def line_length(mesh):
    devices = mesh.devices[:, 0]
    spots = [getattr(device, "coords", None) for device in devices]
    if spots[0] is None:
        return len(spots)
    moved = [k for k in range(3) if len(spots) > 1 and spots[1][k] != spots[0][k]]
    if len(moved) != 1:
        return len(spots)
    count = 1
    while count < len(spots) and all(
        spots[count][k] == spots[0][k] for k in range(3) if k != moved[0]
    ):
        count += 1
    return count


def solution(mesh):
    in_specs = (
        P(None, "rad", "tile", None),
        P("rad", "tile", None),
        P("tile"),
        P("tile"),
        P("tile", None),
        P("tile"),
        P(None, "tile"),
    )
    out_specs = P(None, "rad", "tile", None)
    body = functools.partial(shards, mesh.shape["tile"], mesh.shape["rad"], line_length(mesh))
    return jax.shard_map(body, mesh=mesh, in_specs=in_specs, out_specs=out_specs, check_vma=False)
```

```python
import functools

import jax
import jax.numpy as jnp
from jax import lax
from jax.experimental import pallas as pl
from jax.experimental.pallas import tpu as pltpu
from jax.sharding import PartitionSpec as P

VISCOSITY = 0.1
COUPLING = 1.0
COOL_RATE = 2.0
TIME_STEP = 0.2
MESH = pl.DeviceIdType.MESH
LANES = 128
VMEM_LIMIT = 32 << 20
STEP = 4
EARLY = 3
CROSS = 2
FIRST = 1
NT = (((1,), (1,)), ((), ()))


def in_hbm(x):
    return pltpu.with_memory_space_constraint(x, pltpu.HBM)


def dot(a, b):
    return jnp.dot(a, b, preferred_element_type=jnp.float32)


def split(x):
    high = x.astype(jnp.bfloat16)
    low = (x - high.astype(jnp.float32)).astype(jnp.bfloat16)
    return high, low


def pair_terms(u, ups, downs):
    s1, s2, s3 = [a + b for a, b in zip(ups, downs)]
    d1, d2, d3 = [a - b for a, b in zip(ups, downs)]
    first = (45.0 / 60.0) * d1 - (9.0 / 60.0) * d2 + (1.0 / 60.0) * d3
    second = (
        (270.0 / 180.0) * s1 - (27.0 / 180.0) * s2 + (2.0 / 180.0) * s3 - (490.0 / 180.0) * u
    )
    return first, second


def kernel(
    n_tile, n_rad, inner, cap,
    f4, f2, opacity_in, drow_in, dcol_in, ttile_in, tcell_in, lagrange_in,
    acc,
    x2, ext, edge, relay, ghost, hits, chunks, inc, xall, opsum, oprecv,
    opacity, drow, dcol, ttile, tcell, lagrange,
    x2_sem, in_sem, small_sem, side_sem, rad_sem, far_sem, lvl_send, lvl_recv, row_send, row_recv, hop_recv, fwd_send,
    op_send, op_recv, a2a_send, a2a_recv,
):
    F, L, R, C = acc.shape
    V = F * L
    T = drow.shape[1]
    pack = LANES // cap
    VP = V // pack
    tile = lax.axis_index("tile")
    rad = lax.axis_index("rad")
    quarter = n_tile // 4
    place = lax.rem(tile, inner)
    line = tile // inner

    def each(count, visit):
        if count <= 8:
            for d in range(1, count):
                visit(d)
        else:
            lax.fori_loop(1, count, lambda d, c: (visit(d), c)[1], 0)

    def beside(other):
        across = jnp.abs(lax.rem(other, inner) - place)
        return jnp.logical_and(
            other // inner == line, jnp.logical_or(across == 1, across == inner - 1)
        )

    def count(flag):
        return flag.astype(jnp.int32)

    side_higher = count(place < inner - 1)
    if inner > 2:
        side_higher = side_higher + count(place == 0)

    def signal(semaphore, to_tile, to_rad):
        pl.semaphore_signal(semaphore, inc=1, device_id=(to_tile, to_rad), device_id_type=MESH)

    barrier = pltpu.get_barrier_semaphore()

    def announce_tile(d):
        @pl.when(tile + d < n_tile)
        def _():
            signal(barrier, tile + d, rad)

    def announce_rad(d):
        @pl.when(rad + d < n_rad)
        def _():
            signal(barrier, tile, rad + d)

    each(n_tile, announce_tile)
    each(n_rad, announce_rad)

    halves = C // LANES
    load_x2 = [
        pltpu.make_async_copy(f2.at[:, pl.ds(h * LANES, LANES)], x2.at[h], x2_sem.at[h])
        for h in range(halves)
    ]
    load_small = [
        pltpu.make_async_copy(source, kept, small_sem.at[k])
        for k, (source, kept) in enumerate(
            [
                (dcol_in, dcol), (drow_in, drow), (lagrange_in, lagrange), (ttile_in, ttile),
                (tcell_in, tcell), (opacity_in, opacity),
            ]
        )
    ]
    load_ext = pltpu.make_async_copy(f4, ext.at[:, pl.ds(3, L)], in_sem)
    for copy in load_x2 + load_small:
        copy.start()
    load_ext.start()

    nxt = lax.rem(tile + 1, n_tile)
    prv = lax.rem(tile + n_tile - 1, n_tile)
    has_next = jnp.logical_and(tile != quarter - 1, tile != 3 * quarter - 1)
    has_prev = jnp.logical_and(tile != quarter, tile != 3 * quarter)
    has_above = rad != n_rad - 1
    has_below = rad != 0

    half = F // 2
    relays = inner < n_tile
    crosses = (place == inner - 1, place == 0)
    partner = (nxt, prv)
    via = (tile - (inner - 1), tile + (inner - 1))
    sends = (has_next, has_prev)
    origin = (lax.rem(tile + inner - 1, n_tile), lax.rem(tile + n_tile - inner + 1, n_tile))
    forwards = (
        jnp.logical_and(
            crosses[1],
            jnp.logical_and(origin[0] != quarter - 1, origin[0] != 3 * quarter - 1),
        ),
        jnp.logical_and(
            crosses[0], jnp.logical_and(origin[1] != quarter, origin[1] != 3 * quarter)
        ),
    )
    goal = (lax.rem(origin[0] + 1, n_tile), lax.rem(origin[1] + n_tile - 1, n_tile))
    strip = (pl.ds(R - 3, 3), pl.ds(0, 3))

    def row_copy(f, way):
        return pltpu.make_async_remote_copy(
            src_ref=f4.at[f, :, strip[way]], dst_ref=edge.at[f, :, strip[way]],
            send_sem=row_send.at[f, way], recv_sem=row_recv.at[f, way],
            device_id=(partner[way], rad), device_id_type=MESH,
        )

    def hop_copy(f, way):
        return pltpu.make_async_remote_copy(
            src_ref=f4.at[f, :, strip[way]], dst_ref=relay.at[f - half, :, strip[way]],
            send_sem=row_send.at[f, way], recv_sem=hop_recv.at[f - half, way],
            device_id=(via[way], rad), device_id_type=MESH,
        )

    def forward_copy(f, way):
        return pltpu.make_async_remote_copy(
            src_ref=relay.at[f - half, :, strip[way]], dst_ref=edge.at[f, :, strip[way]],
            send_sem=fwd_send.at[f - half, way], recv_sem=row_recv.at[f, way],
            device_id=(goal[way], rad), device_id_type=MESH,
        )

    def hops(f):
        return relays and f >= half

    def start_hops(way):
        for f in range(half, F):
            if hops(f):
                @pl.when(jnp.logical_and(sends[way], crosses[way]))
                def _():
                    hop_copy(f, way).start()

    def start_beside(way, fields):
        for f in fields:
            @pl.when(jnp.logical_and(sends[way], jnp.logical_not(crosses[way])))
            def _():
                row_copy(f, way).start()

    def start_crossing(fields, lower):
        for f in fields:
            for way in range(2):
                if not hops(f):
                    ready = partner[way] < tile if lower else partner[way] > tile

                    @pl.when(jnp.logical_and(jnp.logical_and(sends[way], crosses[way]), ready))
                    def _():
                        row_copy(f, way).start()

    def forward(f):
        for way in range(2):
            @pl.when(forwards[way])
            def _():
                hop_copy(f, way).wait_recv()
                forward_copy(f, way).start()

    lvl_up = pltpu.make_async_remote_copy(
        src_ref=f4.at[:, pl.ds(L - 3, 3)], dst_ref=ext.at[:, pl.ds(0, 3)],
        send_sem=lvl_send.at[0], recv_sem=lvl_recv.at[0],
        device_id=(tile, lax.rem(rad + 1, n_rad)), device_id_type=MESH,
    )
    lvl_down = pltpu.make_async_remote_copy(
        src_ref=f4.at[:, pl.ds(0, 3)], dst_ref=ext.at[:, pl.ds(L + 3, 3)],
        send_sem=lvl_send.at[1], recv_sem=lvl_recv.at[1],
        device_id=(tile, lax.rem(rad + n_rad - 1, n_rad)), device_id_type=MESH,
    )
    op_copies = [
        pltpu.make_async_remote_copy(
            src_ref=opsum, dst_ref=oprecv.at[d - 1],
            send_sem=op_send.at[d - 1], recv_sem=op_recv.at[d - 1],
            device_id=(tile, lax.rem(rad + d, n_rad)), device_id_type=MESH,
        )
        for d in range(1, n_rad)
    ]

    def await_signals(semaphore, amount):
        @pl.when(amount > 0)
        def _():
            pl.semaphore_wait(semaphore, amount)

    await_signals(barrier, tile + rad)

    def report_tile(d):
        @pl.when(tile >= d)
        def _():
            other = tile - d

            @pl.when(beside(other))
            def _():
                signal(side_sem, other, rad)

            @pl.when(jnp.logical_not(beside(other)))
            def _():
                signal(far_sem, other, rad)

    def report_rad(d):
        @pl.when(rad >= d)
        def _():
            signal(rad_sem, tile, rad - d)

    each(n_tile, report_tile)
    each(n_rad, report_rad)
    start_hops(0)
    start_beside(1, range(EARLY))
    start_crossing(range(CROSS), True)

    @pl.when(has_below)
    def _():
        lvl_down.start()

    await_signals(side_sem, side_higher)
    start_hops(1)
    start_beside(0, range(EARLY))
    await_signals(rad_sem, n_rad - 1 - rad)

    @pl.when(has_above)
    def _():
        lvl_up.start()

    for copy in load_small:
        copy.wait()
    opsum[...] = jnp.sum(opacity[...], axis=0)
    for copy in load_x2:
        copy.wait()

    values = jnp.zeros((V, T), jnp.float32)
    diff = lax.broadcasted_iota(jnp.int32, (C, T), 0) - dcol[...]
    rows = drow[...]
    for r in range(R):
        weights = []
        for b in range(4):
            w = jnp.zeros((1, T), jnp.float32)
            for a in range(4):
                w = jnp.where(rows + a == r, lagrange[4 * a + b : 4 * a + b + 1, :], w)
            weights.append(w)
        g = jnp.where(diff == 0, weights[0], 0.0)
        for b in range(1, 4):
            g = jnp.where(diff == b, weights[b], g)
        gh, gl = split(g)
        xh, xl = split(
            jnp.concatenate([x2[h, pl.ds(r, V, stride=R), :] for h in range(halves)], axis=1)
        )
        values = values + (dot(xh, gh) + (dot(xl, gh) + dot(xh, gl)))

    target = ttile[...]
    kinds = max(16, n_tile)
    hot = (lax.broadcasted_iota(jnp.int32, (kinds, T), 0) == target).astype(jnp.float32)
    before = (
        lax.broadcasted_iota(jnp.int32, (T, T), 0) < lax.broadcasted_iota(jnp.int32, (T, T), 1)
    ).astype(jnp.float32)
    earlier = dot(hot.astype(jnp.bfloat16), before.astype(jnp.bfloat16))
    rank = jnp.sum(earlier * hot, axis=0, keepdims=True)
    key = target * cap + rank.astype(jnp.int32)
    lane_slot = lax.rem(lax.broadcasted_iota(jnp.int32, (LANES, T), 0), cap)
    vh, vl = split(values)
    label = tcell[...]
    side = lax.broadcasted_iota(jnp.int32, (16, T), 0)
    label = jnp.where(
        side == 0, label // C + 1, jnp.where(side == 1, lax.rem(label, C), 0)
    ).astype(jnp.float32).astype(jnp.bfloat16)
    stacked = jnp.concatenate([vh, vl, label], axis=0)
    lane_group = lax.broadcasted_iota(jnp.int32, (VP, LANES), 1) // cap

    def chunk(d):
        first = lax.rem(tile + d, n_tile) * cap
        chosen = (key == lane_slot + first).astype(jnp.float32).astype(jnp.bfloat16)
        moved = lax.dot_general(stacked, chosen, NT, preferred_element_type=jnp.float32)
        full = moved[:V] + moved[V : 2 * V]
        picked = full[:VP]
        for g in range(1, pack):
            picked = jnp.where(lane_group == g, full[g * VP : (g + 1) * VP], picked)
        return picked, moved[2 * V : 2 * V + 8]

    await_signals(far_sem, n_tile - 1 - tile - side_higher)
    start_crossing(range(CROSS), False)

    picked, marks = chunk(0)
    inc[0, pl.ds(0, VP)] = picked
    inc[0, pl.ds(VP, 8)] = marks
    used = pl.ds(0, VP + 2)

    def a2a_copy(d):
        return pltpu.make_async_remote_copy(
            src_ref=chunks.at[d, used], dst_ref=inc.at[d, used],
            send_sem=a2a_send.at[d], recv_sem=a2a_recv.at[d],
            device_id=(lax.rem(tile + d, n_tile), rad), device_id_type=MESH,
        )

    def fill_chunk(d):
        picked, marks = chunk(d)
        chunks[d, pl.ds(0, VP)] = picked
        chunks[d, pl.ds(VP, 8)] = marks

    each(n_tile, fill_chunk)
    each(n_tile, lambda d: a2a_copy(d).start())
    for copy in op_copies:
        copy.start()
    start_crossing(range(CROSS, F), True)
    start_crossing(range(CROSS, F), False)
    start_beside(1, range(EARLY, F))
    start_beside(0, range(EARLY, F))

    load_ext.wait()
    zeros3 = jnp.zeros((F, 3, R, C), jnp.float32)

    @pl.when(has_below)
    def _():
        lvl_up.wait_recv()

    @pl.when(jnp.logical_not(has_below))
    def _():
        ext[:, pl.ds(0, 3)] = zeros3

    @pl.when(has_above)
    def _():
        lvl_down.wait_recv()

    @pl.when(jnp.logical_not(has_above))
    def _():
        ext[:, pl.ds(L + 3, 3)] = zeros3

    no_rows = jnp.zeros((F, L, 3, C), jnp.float32)

    @pl.when(jnp.logical_not(has_prev))
    def _():
        edge[:, :, strip[0]] = no_rows

    @pl.when(jnp.logical_not(has_next))
    def _():
        edge[:, :, strip[1]] = no_rows

    column = lax.broadcasted_iota(jnp.int32, (STEP, R, C), 2)

    def local_part(f, i, carry):
        l = i * STEP
        u = ext[f, pl.ds(l + 3, STEP)]
        speed1 = ext[1, pl.ds(l + 3, STEP)]
        speed3 = ext[3, pl.ds(l + 3, STEP)]
        ups = [ext[f, pl.ds(l + 3 + k, STEP)] for k in (1, 2, 3)]
        downs = [ext[f, pl.ds(l + 3 - k, STEP)] for k in (1, 2, 3)]
        first, second = pair_terms(u, ups, downs)
        total = VISCOSITY * second - speed1 * first
        ups = [jnp.where(column < C - k, pltpu.roll(u, C - k, 2), 0.0) for k in (1, 2, 3)]
        downs = [jnp.where(column >= k, pltpu.roll(u, k, 2), 0.0) for k in (1, 2, 3)]
        first, second = pair_terms(u, ups, downs)
        acc[f, pl.ds(l, STEP)] = total + (VISCOSITY * second - speed3 * first)
        return carry

    for f in range(F):
        lax.fori_loop(0, L // STEP, functools.partial(local_part, f), 0)
        if relays and FIRST <= f < FIRST + F - half:
            forward(half + f - FIRST)

    above = jnp.zeros((R, C), jnp.float32)
    for d in range(1, n_rad):
        op_copies[d - 1].wait_recv()
        above = above + jnp.where(rad >= d, oprecv[d - 1], 0.0)

    def cool(l, so_far):
        mine = opacity[l]
        depth = so_far + 0.5 * mine
        acc[7, l] = acc[7, l] - COOL_RATE * jnp.exp(-depth) * ext[7, l + 3]
        return so_far + mine

    lax.fori_loop(0, L, cool, above)

    for d in range(1, n_tile):
        a2a_copy(d).wait_recv()
    group_of = lax.broadcasted_iota(jnp.int32, (1, LANES), 1) // cap
    row_marks = []
    column_marks = []
    for d0 in range(0, n_tile, pack):
        lanes = pl.ds(d0 // pack * LANES, LANES)
        parts = [inc[d0 + j] for j in range(pack)]
        for g in range(pack):
            joined = None
            for j in range(pack):
                part = parts[j][:VP]
                turn = ((j - g) * cap) % LANES
                if turn:
                    part = pltpu.roll(part, turn, 1)
                joined = part if joined is None else jnp.where(lane_group == j, part, joined)
            high, low = split(joined)
            xall[pl.ds(g * VP, VP), lanes] = high
            xall[pl.ds(V + g * VP, VP), lanes] = low
        xall[pl.ds(2 * V, 16), lanes] = jnp.ones((16, LANES), jnp.bfloat16)
        row_mark = parts[0][VP : VP + 1]
        column_mark = parts[0][VP + 1 : VP + 2]
        for j in range(1, pack):
            row_mark = jnp.where(group_of == j, parts[j][VP : VP + 1], row_mark)
            column_mark = jnp.where(group_of == j, parts[j][VP + 1 : VP + 2], column_mark)
        row_marks.append(row_mark)
        column_marks.append(column_mark)
    row_mark = jnp.concatenate(row_marks, axis=1).astype(jnp.int32)
    column_mark = jnp.concatenate(column_marks, axis=1).astype(jnp.int32)
    slots = n_tile * cap
    cell_column = lax.broadcasted_iota(jnp.int32, (C, slots), 0)
    everything = xall[...]
    for r in range(R):
        wanted = jnp.where(row_mark == r + 1, column_mark, -1)
        place = (cell_column == wanted).astype(jnp.float32).astype(jnp.bfloat16)
        got = lax.dot_general(everything, place, NT, preferred_element_type=jnp.float32)
        total = got[:V] + got[V : 2 * V]
        for h in range(halves):
            ghost[h, pl.ds(r, V, stride=R), :] = total[:, h * LANES : (h + 1) * LANES]
        hits[pl.ds(r, 1), :] = got[2 * V : 2 * V + 1]

    row = lax.broadcasted_iota(jnp.int32, (STEP, R, C), 1)

    for f in range(F):
        @pl.when(has_prev)
        def _():
            row_copy(f, 0).wait_recv()

        @pl.when(has_next)
        def _():
            row_copy(f, 1).wait_recv()

        def row_part(i, carry):
            l = i * STEP
            u = ext[f, pl.ds(l + 3, STEP)]
            speed2 = ext[2, pl.ds(l + 3, STEP)]
            at = pl.ds(pl.multiple_of((f * L + l) * R, STEP * R), STEP * R)
            rim = edge[f, pl.ds(l, STEP)]
            arrived = jnp.concatenate(
                [ghost[h, at, :].reshape(STEP, R, LANES) for h in range(halves)], axis=2
            )
            ups = [pltpu.roll(jnp.where(row < k, rim, u), R - k, 1) for k in (1, 2, 3)]
            downs = [pltpu.roll(jnp.where(row >= R - k, rim, u), k, 1) for k in (1, 2, 3)]
            first, second = pair_terms(u, ups, downs)
            total = acc[f, pl.ds(l, STEP)] + (VISCOSITY * second - speed2 * first)
            total = total + COUPLING * (arrived - hits[...] * u)
            acc[f, pl.ds(l, STEP)] = u + TIME_STEP * total
            return carry

        lax.fori_loop(0, L // STEP, row_part, 0)

    @pl.when(has_above)
    def _():
        lvl_up.wait_send()

    @pl.when(has_below)
    def _():
        lvl_down.wait_send()

    for copy in op_copies:
        copy.wait_send()
    for d in range(1, n_tile):
        a2a_copy(d).wait_send()
    for f in range(F):
        for way in range(2):
            @pl.when(sends[way])
            def _():
                row_copy(f, way).wait_send()

            if hops(f):
                @pl.when(forwards[way])
                def _():
                    forward_copy(f, way).wait_send()


def shards(n_tile, n_rad, inner, fields, opacity, donor_row, donor_column, target_tile, target_cell, lagrange):
    F, L, R, C = fields.shape
    V = F * L
    T = donor_row.shape[0]
    cap = max(16, 2 * T // n_tile)
    pack = LANES // cap
    VP = V // pack
    hbm = pl.BlockSpec(memory_space=pltpu.HBM)
    vmem = pl.BlockSpec(memory_space=pltpu.VMEM)
    dma = pltpu.SemaphoreType.DMA
    f32 = jnp.float32
    return pl.pallas_call(
        functools.partial(kernel, n_tile, n_rad, inner, cap),
        out_shape=pltpu.VMEM(fields.shape, f32),
        in_specs=[hbm] * 8,
        out_specs=vmem,
        scratch_shapes=[
            pltpu.VMEM((C // LANES, V * R, LANES), f32),
            pltpu.VMEM((F, L + 6, R, C), f32),
            pltpu.VMEM((F, L, R, C), f32),
            pltpu.VMEM((F - F // 2, L, R, C), f32),
            pltpu.VMEM((C // LANES, V * R, LANES), f32),
            pltpu.VMEM((R, C), f32),
            pltpu.VMEM((n_tile, VP + 8, LANES), f32),
            pltpu.VMEM((n_tile, VP + 8, LANES), f32),
            pltpu.VMEM((2 * V + 16, n_tile * cap), jnp.bfloat16),
            pltpu.VMEM((R, C), f32),
            pltpu.VMEM((n_rad - 1, R, C), f32),
            pltpu.VMEM((L, R, C), f32),
            pltpu.VMEM((1, T), jnp.int32),
            pltpu.VMEM((1, T), jnp.int32),
            pltpu.VMEM((1, T), jnp.int32),
            pltpu.VMEM((1, T), jnp.int32),
            pltpu.VMEM(lagrange.shape, f32),
            dma((C // LANES,)),
            dma(()),
            dma((6,)),
            pltpu.SemaphoreType.REGULAR,
            pltpu.SemaphoreType.REGULAR,
            pltpu.SemaphoreType.REGULAR,
            dma((2,)),
            dma((2,)),
            dma((F, 2)),
            dma((F, 2)),
            dma((F - F // 2, 2)),
            dma((F - F // 2, 2)),
            dma((n_rad - 1,)),
            dma((n_rad - 1,)),
            dma((n_tile,)),
            dma((n_tile,)),
        ],
        compiler_params=pltpu.CompilerParams(
            collective_id=0, has_side_effects=True, vmem_limit_bytes=VMEM_LIMIT
        ),
    )(
        in_hbm(fields),
        in_hbm(fields.reshape(V * R, C)),
        in_hbm(opacity),
        in_hbm(donor_row.reshape(1, T)),
        in_hbm(donor_column.reshape(1, T)),
        in_hbm(target_tile.reshape(1, T)),
        in_hbm(target_cell.reshape(1, T)),
        in_hbm(lagrange),
    )


def line_length(mesh):
    devices = mesh.devices[:, 0]
    spots = [getattr(device, "coords", None) for device in devices]
    if spots[0] is None:
        return len(spots)
    moved = [k for k in range(3) if len(spots) > 1 and spots[1][k] != spots[0][k]]
    if len(moved) != 1:
        return len(spots)
    count = 1
    while count < len(spots) and all(
        spots[count][k] == spots[0][k] for k in range(3) if k != moved[0]
    ):
        count += 1
    return count


def solution(mesh):
    in_specs = (
        P(None, "rad", "tile", None),
        P("rad", "tile", None),
        P("tile"),
        P("tile"),
        P("tile", None),
        P("tile"),
        P(None, "tile"),
    )
    out_specs = P(None, "rad", "tile", None)
    body = functools.partial(shards, mesh.shape["tile"], mesh.shape["rad"], line_length(mesh))
    return jax.shard_map(body, mesh=mesh, in_specs=in_specs, out_specs=out_specs, check_vma=False)
```

```python
import functools

import jax
import jax.numpy as jnp
from jax import lax
from jax.experimental import pallas as pl
from jax.experimental.pallas import tpu as pltpu
from jax.sharding import PartitionSpec as P

VISCOSITY = 0.1
COUPLING = 1.0
COOL_RATE = 2.0
TIME_STEP = 0.2
MESH = pl.DeviceIdType.MESH
LANES = 128
VMEM_LIMIT = 32 << 20
STEP = 4
EARLY = 3
CROSS = 2
MORE = 2
FEWER = 2
SOON = 2
ORDER = (0, 1, 4, 5, 6, 2, 3, 7)
FIRST = 1
NT = (((1,), (1,)), ((), ()))


def in_hbm(x):
    return pltpu.with_memory_space_constraint(x, pltpu.HBM)


def dot(a, b):
    return jnp.dot(a, b, preferred_element_type=jnp.float32)


def split(x):
    high = x.astype(jnp.bfloat16)
    low = (x - high.astype(jnp.float32)).astype(jnp.bfloat16)
    return high, low


def pair_terms(u, ups, downs):
    s1, s2, s3 = [a + b for a, b in zip(ups, downs)]
    d1, d2, d3 = [a - b for a, b in zip(ups, downs)]
    first = (45.0 / 60.0) * d1 - (9.0 / 60.0) * d2 + (1.0 / 60.0) * d3
    second = (
        (270.0 / 180.0) * s1 - (27.0 / 180.0) * s2 + (2.0 / 180.0) * s3 - (490.0 / 180.0) * u
    )
    return first, second


def kernel(
    n_tile, n_rad, inner, cap,
    f4, f2, opacity_in, drow_in, dcol_in, ttile_in, tcell_in, lagrange_in,
    acc,
    x2, ext, edge, relay, ghost, hits, chunks, inc, xall, opsum, oprecv,
    opacity, drow, dcol, ttile, tcell, lagrange,
    x2_sem, in_sem, small_sem, side_sem, turn_sem, rad_sem, far_sem, lvl_send, lvl_recv, row_send, row_recv, hop_recv, fwd_send,
    op_send, op_recv, a2a_send, a2a_recv,
):
    F, L, R, C = acc.shape
    V = F * L
    T = drow.shape[1]
    pack = LANES // cap
    VP = V // pack
    tile = lax.axis_index("tile")
    rad = lax.axis_index("rad")
    quarter = n_tile // 4
    place = lax.rem(tile, inner)
    line = tile // inner

    def each(count, visit):
        if count <= 8:
            for d in range(1, count):
                visit(d)
        else:
            lax.fori_loop(1, count, lambda d, c: (visit(d), c)[1], 0)

    def beside(other):
        across = jnp.abs(lax.rem(other, inner) - place)
        return jnp.logical_and(
            other // inner == line, jnp.logical_or(across == 1, across == inner - 1)
        )

    def count(flag):
        return flag.astype(jnp.int32)

    side_higher = count(place < inner - 1)
    turn_higher = count(jnp.logical_and(place == inner - 1, tile < n_tile - 1))
    if inner > 2:
        side_higher = side_higher + count(place == 0)

    def signal(semaphore, to_tile, to_rad):
        pl.semaphore_signal(semaphore, inc=1, device_id=(to_tile, to_rad), device_id_type=MESH)

    barrier = pltpu.get_barrier_semaphore()

    def announce_tile(d):
        @pl.when(tile + d < n_tile)
        def _():
            signal(barrier, tile + d, rad)

    def announce_rad(d):
        @pl.when(rad + d < n_rad)
        def _():
            signal(barrier, tile, rad + d)

    each(n_tile, announce_tile)
    each(n_rad, announce_rad)

    halves = C // LANES
    load_x2 = [
        pltpu.make_async_copy(f2.at[:, pl.ds(h * LANES, LANES)], x2.at[h], x2_sem.at[h])
        for h in range(halves)
    ]
    load_small = [
        pltpu.make_async_copy(source, kept, small_sem.at[k])
        for k, (source, kept) in enumerate(
            [
                (dcol_in, dcol), (drow_in, drow), (lagrange_in, lagrange), (ttile_in, ttile),
                (tcell_in, tcell), (opacity_in, opacity),
            ]
        )
    ]
    load_ext = pltpu.make_async_copy(f4, ext.at[:, pl.ds(3, L)], in_sem)
    for copy in load_x2 + load_small:
        copy.start()
    load_ext.start()

    nxt = lax.rem(tile + 1, n_tile)
    prv = lax.rem(tile + n_tile - 1, n_tile)
    has_next = jnp.logical_and(tile != quarter - 1, tile != 3 * quarter - 1)
    has_prev = jnp.logical_and(tile != quarter, tile != 3 * quarter)
    has_above = rad != n_rad - 1
    has_below = rad != 0

    half = F // 2
    relays = inner < n_tile
    order = [f for f in ORDER if f < F] if F == len(ORDER) else list(range(F))
    whole = [f for f in order if f < half or f == F - 1 or not relays]
    crosses = (place == inner - 1, place == 0)
    partner = (nxt, prv)
    via = (tile - (inner - 1), tile + (inner - 1))
    sends = (has_next, has_prev)
    origin = (lax.rem(tile + inner - 1, n_tile), lax.rem(tile + n_tile - inner + 1, n_tile))
    forwards = (
        jnp.logical_and(
            crosses[1],
            jnp.logical_and(origin[0] != quarter - 1, origin[0] != 3 * quarter - 1),
        ),
        jnp.logical_and(
            crosses[0], jnp.logical_and(origin[1] != quarter, origin[1] != 3 * quarter)
        ),
    )
    goal = (lax.rem(origin[0] + 1, n_tile), lax.rem(origin[1] + n_tile - 1, n_tile))
    strip = (pl.ds(R - 3, 3), pl.ds(0, 3))

    def row_copy(f, way):
        return pltpu.make_async_remote_copy(
            src_ref=f4.at[f, :, strip[way]], dst_ref=edge.at[f, :, strip[way]],
            send_sem=row_send.at[f, way], recv_sem=row_recv.at[f, way],
            device_id=(partner[way], rad), device_id_type=MESH,
        )

    def hop_copy(f, way):
        return pltpu.make_async_remote_copy(
            src_ref=f4.at[f, :, strip[way]], dst_ref=relay.at[f - shared, :, strip[way]],
            send_sem=row_send.at[f, way], recv_sem=hop_recv.at[f - shared, way],
            device_id=(via[way], rad), device_id_type=MESH,
        )

    def forward_copy(f, way):
        return pltpu.make_async_remote_copy(
            src_ref=relay.at[f - shared, :, strip[way]], dst_ref=edge.at[f, :, strip[way]],
            send_sem=fwd_send.at[f - shared, way], recv_sem=row_recv.at[f, way],
            device_id=(goal[way], rad), device_id_type=MESH,
        )

    shared = half - 1
    relayed = [*range(half, F), shared] if relays else []
    def by_relay(f, way, source):
        wraps = source == n_tile - 1
        if f == shared and way == 0 and relays:
            return jnp.logical_and(wraps, lax.rem(rad, MORE) == 0)
        if f == F - 1 and way == 0 and relays:
            return jnp.logical_or(wraps, lax.rem(rad, FEWER) != 0)
        return jnp.logical_and(tile >= 0, f in relayed and f != shared)

    def start_hops(way):
        for f in relayed:
            through = by_relay(f, way, tile)

            @pl.when(jnp.logical_and(jnp.logical_and(sends[way], crosses[way]), through))
            def _():
                hop_copy(f, way).start()

    def start_beside(way, fields):
        for f in fields:
            @pl.when(jnp.logical_and(sends[way], jnp.logical_not(crosses[way])))
            def _():
                row_copy(f, way).start()

    def start_crossing(fields, way, ready):
        for f in fields:
            direct = jnp.logical_and(ready, jnp.logical_not(by_relay(f, way, tile)))

            @pl.when(jnp.logical_and(jnp.logical_and(sends[way], crosses[way]), direct))
            def _():
                row_copy(f, way).start()

    def forward(f):
        for way in range(2):
            @pl.when(jnp.logical_and(forwards[way], by_relay(f, way, origin[way])))
            def _():
                hop_copy(f, way).wait_recv()
                forward_copy(f, way).start()

    lvl_up = pltpu.make_async_remote_copy(
        src_ref=f4.at[:, pl.ds(L - 3, 3)], dst_ref=ext.at[:, pl.ds(0, 3)],
        send_sem=lvl_send.at[0], recv_sem=lvl_recv.at[0],
        device_id=(tile, lax.rem(rad + 1, n_rad)), device_id_type=MESH,
    )
    lvl_down = pltpu.make_async_remote_copy(
        src_ref=f4.at[:, pl.ds(0, 3)], dst_ref=ext.at[:, pl.ds(L + 3, 3)],
        send_sem=lvl_send.at[1], recv_sem=lvl_recv.at[1],
        device_id=(tile, lax.rem(rad + n_rad - 1, n_rad)), device_id_type=MESH,
    )
    op_copies = [
        pltpu.make_async_remote_copy(
            src_ref=opsum, dst_ref=oprecv.at[d - 1],
            send_sem=op_send.at[d - 1], recv_sem=op_recv.at[d - 1],
            device_id=(tile, lax.rem(rad + d, n_rad)), device_id_type=MESH,
        )
        for d in range(1, n_rad)
    ]

    def await_signals(semaphore, amount):
        @pl.when(amount > 0)
        def _():
            pl.semaphore_wait(semaphore, amount)

    await_signals(barrier, tile + rad)

    def report_tile(d):
        @pl.when(tile >= d)
        def _():
            other = tile - d

            after = jnp.logical_and(place == 0, d == 1)

            @pl.when(beside(other))
            def _():
                signal(side_sem, other, rad)

            @pl.when(after)
            def _():
                signal(turn_sem, other, rad)

            @pl.when(jnp.logical_not(jnp.logical_or(beside(other), after)))
            def _():
                signal(far_sem, other, rad)

    def report_rad(d):
        @pl.when(rad >= d)
        def _():
            signal(rad_sem, tile, rad - d)

    each(n_tile, report_tile)
    each(n_rad, report_rad)
    start_hops(0)
    start_beside(1, order[:EARLY])
    start_crossing(whole[:CROSS], 0, nxt < tile)
    start_crossing(whole[:CROSS], 1, prv < tile)

    @pl.when(has_below)
    def _():
        lvl_down.start()

    await_signals(side_sem, side_higher)
    start_hops(1)
    start_beside(0, order[:EARLY])
    await_signals(turn_sem, turn_higher)
    start_crossing(whole[:CROSS], 0, nxt > tile)
    await_signals(rad_sem, n_rad - 1 - rad)

    @pl.when(has_above)
    def _():
        lvl_up.start()

    for copy in load_small:
        copy.wait()
    opsum[...] = jnp.sum(opacity[...], axis=0)
    for copy in load_x2:
        copy.wait()

    values = jnp.zeros((V, T), jnp.float32)
    diff = lax.broadcasted_iota(jnp.int32, (C, T), 0) - dcol[...]
    rows = drow[...]
    for r in range(R):
        weights = []
        for b in range(4):
            w = jnp.zeros((1, T), jnp.float32)
            for a in range(4):
                w = jnp.where(rows + a == r, lagrange[4 * a + b : 4 * a + b + 1, :], w)
            weights.append(w)
        g = jnp.where(diff == 0, weights[0], 0.0)
        for b in range(1, 4):
            g = jnp.where(diff == b, weights[b], g)
        gh, gl = split(g)
        xh, xl = split(
            jnp.concatenate([x2[h, pl.ds(r, V, stride=R), :] for h in range(halves)], axis=1)
        )
        values = values + (dot(xh, gh) + (dot(xl, gh) + dot(xh, gl)))

    target = ttile[...]
    kinds = max(16, n_tile)
    hot = (lax.broadcasted_iota(jnp.int32, (kinds, T), 0) == target).astype(jnp.float32)
    before = (
        lax.broadcasted_iota(jnp.int32, (T, T), 0) < lax.broadcasted_iota(jnp.int32, (T, T), 1)
    ).astype(jnp.float32)
    earlier = dot(hot.astype(jnp.bfloat16), before.astype(jnp.bfloat16))
    rank = jnp.sum(earlier * hot, axis=0, keepdims=True)
    key = target * cap + rank.astype(jnp.int32)
    lane_slot = lax.rem(lax.broadcasted_iota(jnp.int32, (LANES, T), 0), cap)
    vh, vl = split(values)
    label = tcell[...]
    side = lax.broadcasted_iota(jnp.int32, (16, T), 0)
    label = jnp.where(
        side == 0, label // C + 1, jnp.where(side == 1, lax.rem(label, C), 0)
    ).astype(jnp.float32).astype(jnp.bfloat16)
    stacked = jnp.concatenate([vh, vl, label], axis=0)
    lane_group = lax.broadcasted_iota(jnp.int32, (VP, LANES), 1) // cap

    def chunk(d):
        first = lax.rem(tile + d, n_tile) * cap
        chosen = (key == lane_slot + first).astype(jnp.float32).astype(jnp.bfloat16)
        moved = lax.dot_general(stacked, chosen, NT, preferred_element_type=jnp.float32)
        full = moved[:V] + moved[V : 2 * V]
        picked = full[:VP]
        for g in range(1, pack):
            picked = jnp.where(lane_group == g, full[g * VP : (g + 1) * VP], picked)
        return picked, moved[2 * V : 2 * V + 8]

    await_signals(far_sem, n_tile - 1 - tile - side_higher - turn_higher)
    start_crossing(whole[:CROSS], 1, prv > tile)
    if relays:
        for f in relayed[:SOON]:
            forward(f)

    picked, marks = chunk(0)
    inc[0, pl.ds(0, VP)] = picked
    inc[0, pl.ds(VP, 8)] = marks
    used = pl.ds(0, VP + 2)

    def a2a_copy(d):
        return pltpu.make_async_remote_copy(
            src_ref=chunks.at[d, used], dst_ref=inc.at[d, used],
            send_sem=a2a_send.at[d], recv_sem=a2a_recv.at[d],
            device_id=(lax.rem(tile + d, n_tile), rad), device_id_type=MESH,
        )

    def fill_chunk(d):
        picked, marks = chunk(d)
        chunks[d, pl.ds(0, VP)] = picked
        chunks[d, pl.ds(VP, 8)] = marks

    if n_tile <= 8:
        turns = sorted(range(1, n_tile), key=lambda d: abs(2 * d - n_tile))
        for k, d in enumerate(turns):
            fill_chunk(d)
            if k:
                a2a_copy(turns[k - 1]).start()
        a2a_copy(turns[-1]).start()
    else:
        each(n_tile, fill_chunk)
        each(n_tile, lambda d: a2a_copy(d).start())
    for copy in op_copies:
        copy.start()
    start_crossing(whole[CROSS:], 0, tile >= 0)
    start_crossing(whole[CROSS:], 1, tile >= 0)
    start_beside(1, order[EARLY:])
    start_beside(0, order[EARLY:])

    load_ext.wait()
    zeros3 = jnp.zeros((F, 3, R, C), jnp.float32)

    @pl.when(has_below)
    def _():
        lvl_up.wait_recv()

    @pl.when(jnp.logical_not(has_below))
    def _():
        ext[:, pl.ds(0, 3)] = zeros3

    @pl.when(has_above)
    def _():
        lvl_down.wait_recv()

    @pl.when(jnp.logical_not(has_above))
    def _():
        ext[:, pl.ds(L + 3, 3)] = zeros3

    no_rows = jnp.zeros((F, L, 3, C), jnp.float32)

    @pl.when(jnp.logical_not(has_prev))
    def _():
        edge[:, :, strip[0]] = no_rows

    @pl.when(jnp.logical_not(has_next))
    def _():
        edge[:, :, strip[1]] = no_rows

    column = lax.broadcasted_iota(jnp.int32, (STEP, R, C), 2)

    def local_part(f, i, carry):
        l = i * STEP
        u = ext[f, pl.ds(l + 3, STEP)]
        speed1 = ext[1, pl.ds(l + 3, STEP)]
        speed3 = ext[3, pl.ds(l + 3, STEP)]
        ups = [ext[f, pl.ds(l + 3 + k, STEP)] for k in (1, 2, 3)]
        downs = [ext[f, pl.ds(l + 3 - k, STEP)] for k in (1, 2, 3)]
        first, second = pair_terms(u, ups, downs)
        total = VISCOSITY * second - speed1 * first
        ups = [jnp.where(column < C - k, pltpu.roll(u, C - k, 2), 0.0) for k in (1, 2, 3)]
        downs = [jnp.where(column >= k, pltpu.roll(u, k, 2), 0.0) for k in (1, 2, 3)]
        first, second = pair_terms(u, ups, downs)
        acc[f, pl.ds(l, STEP)] = total + (VISCOSITY * second - speed3 * first)
        return carry

    for f in range(F):
        lax.fori_loop(0, L // STEP, functools.partial(local_part, f), 0)
        if f >= FIRST:
            for g in relayed[SOON + f - FIRST : SOON + f - FIRST + 1]:
                forward(g)

    above = jnp.zeros((R, C), jnp.float32)
    for d in range(1, n_rad):
        op_copies[d - 1].wait_recv()
        above = above + jnp.where(rad >= d, oprecv[d - 1], 0.0)

    def cool(l, so_far):
        mine = opacity[l]
        depth = so_far + 0.5 * mine
        acc[7, l] = acc[7, l] - COOL_RATE * jnp.exp(-depth) * ext[7, l + 3]
        return so_far + mine

    lax.fori_loop(0, L, cool, above)

    for d in range(1, n_tile):
        a2a_copy(d).wait_recv()
    group_of = lax.broadcasted_iota(jnp.int32, (1, LANES), 1) // cap
    row_marks = []
    column_marks = []
    for d0 in range(0, n_tile, pack):
        lanes = pl.ds(d0 // pack * LANES, LANES)
        parts = [inc[d0 + j] for j in range(pack)]
        for g in range(pack):
            joined = None
            for j in range(pack):
                part = parts[j][:VP]
                turn = ((j - g) * cap) % LANES
                if turn:
                    part = pltpu.roll(part, turn, 1)
                joined = part if joined is None else jnp.where(lane_group == j, part, joined)
            high, low = split(joined)
            xall[pl.ds(g * VP, VP), lanes] = high
            xall[pl.ds(V + g * VP, VP), lanes] = low
        xall[pl.ds(2 * V, 16), lanes] = jnp.ones((16, LANES), jnp.bfloat16)
        row_mark = parts[0][VP : VP + 1]
        column_mark = parts[0][VP + 1 : VP + 2]
        for j in range(1, pack):
            row_mark = jnp.where(group_of == j, parts[j][VP : VP + 1], row_mark)
            column_mark = jnp.where(group_of == j, parts[j][VP + 1 : VP + 2], column_mark)
        row_marks.append(row_mark)
        column_marks.append(column_mark)
    row_mark = jnp.concatenate(row_marks, axis=1).astype(jnp.int32)
    column_mark = jnp.concatenate(column_marks, axis=1).astype(jnp.int32)
    slots = n_tile * cap
    cell_column = lax.broadcasted_iota(jnp.int32, (C, slots), 0)
    everything = xall[...]
    for r in range(R):
        wanted = jnp.where(row_mark == r + 1, column_mark, -1)
        place = (cell_column == wanted).astype(jnp.float32).astype(jnp.bfloat16)
        got = lax.dot_general(everything, place, NT, preferred_element_type=jnp.float32)
        total = got[:V] + got[V : 2 * V]
        for h in range(halves):
            ghost[h, pl.ds(r, V, stride=R), :] = total[:, h * LANES : (h + 1) * LANES]
        hits[pl.ds(r, 1), :] = got[2 * V : 2 * V + 1]

    row = lax.broadcasted_iota(jnp.int32, (STEP, R, C), 1)

    for f in order:
        @pl.when(has_prev)
        def _():
            row_copy(f, 0).wait_recv()

        @pl.when(has_next)
        def _():
            row_copy(f, 1).wait_recv()

        def row_part(i, carry):
            l = i * STEP
            u = ext[f, pl.ds(l + 3, STEP)]
            speed2 = ext[2, pl.ds(l + 3, STEP)]
            at = pl.ds(pl.multiple_of((f * L + l) * R, STEP * R), STEP * R)
            rim = edge[f, pl.ds(l, STEP)]
            arrived = jnp.concatenate(
                [ghost[h, at, :].reshape(STEP, R, LANES) for h in range(halves)], axis=2
            )
            ups = [pltpu.roll(jnp.where(row < k, rim, u), R - k, 1) for k in (1, 2, 3)]
            downs = [pltpu.roll(jnp.where(row >= R - k, rim, u), k, 1) for k in (1, 2, 3)]
            first, second = pair_terms(u, ups, downs)
            total = acc[f, pl.ds(l, STEP)] + (VISCOSITY * second - speed2 * first)
            total = total + COUPLING * (arrived - hits[...] * u)
            acc[f, pl.ds(l, STEP)] = u + TIME_STEP * total
            return carry

        lax.fori_loop(0, L // STEP, row_part, 0)

    @pl.when(has_above)
    def _():
        lvl_up.wait_send()

    @pl.when(has_below)
    def _():
        lvl_down.wait_send()

    for copy in op_copies:
        copy.wait_send()
    for d in range(1, n_tile):
        a2a_copy(d).wait_send()
    for f in range(F):
        for way in range(2):
            @pl.when(sends[way])
            def _():
                row_copy(f, way).wait_send()

            if f in relayed:
                @pl.when(jnp.logical_and(forwards[way], by_relay(f, way, origin[way])))
                def _():
                    forward_copy(f, way).wait_send()


def shards(n_tile, n_rad, inner, fields, opacity, donor_row, donor_column, target_tile, target_cell, lagrange):
    F, L, R, C = fields.shape
    V = F * L
    T = donor_row.shape[0]
    cap = max(16, 2 * T // n_tile)
    pack = LANES // cap
    VP = V // pack
    hbm = pl.BlockSpec(memory_space=pltpu.HBM)
    vmem = pl.BlockSpec(memory_space=pltpu.VMEM)
    dma = pltpu.SemaphoreType.DMA
    f32 = jnp.float32
    return pl.pallas_call(
        functools.partial(kernel, n_tile, n_rad, inner, cap),
        out_shape=pltpu.VMEM(fields.shape, f32),
        in_specs=[hbm] * 8,
        out_specs=vmem,
        scratch_shapes=[
            pltpu.VMEM((C // LANES, V * R, LANES), f32),
            pltpu.VMEM((F, L + 6, R, C), f32),
            pltpu.VMEM((F, L, R, C), f32),
            pltpu.VMEM((F - F // 2 + 1, L, R, C), f32),
            pltpu.VMEM((C // LANES, V * R, LANES), f32),
            pltpu.VMEM((R, C), f32),
            pltpu.VMEM((n_tile, VP + 8, LANES), f32),
            pltpu.VMEM((n_tile, VP + 8, LANES), f32),
            pltpu.VMEM((2 * V + 16, n_tile * cap), jnp.bfloat16),
            pltpu.VMEM((R, C), f32),
            pltpu.VMEM((n_rad - 1, R, C), f32),
            pltpu.VMEM((L, R, C), f32),
            pltpu.VMEM((1, T), jnp.int32),
            pltpu.VMEM((1, T), jnp.int32),
            pltpu.VMEM((1, T), jnp.int32),
            pltpu.VMEM((1, T), jnp.int32),
            pltpu.VMEM(lagrange.shape, f32),
            dma((C // LANES,)),
            dma(()),
            dma((6,)),
            pltpu.SemaphoreType.REGULAR,
            pltpu.SemaphoreType.REGULAR,
            pltpu.SemaphoreType.REGULAR,
            pltpu.SemaphoreType.REGULAR,
            dma((2,)),
            dma((2,)),
            dma((F, 2)),
            dma((F, 2)),
            dma((F - F // 2 + 1, 2)),
            dma((F - F // 2 + 1, 2)),
            dma((n_rad - 1,)),
            dma((n_rad - 1,)),
            dma((n_tile,)),
            dma((n_tile,)),
        ],
        compiler_params=pltpu.CompilerParams(
            collective_id=0, has_side_effects=True, vmem_limit_bytes=VMEM_LIMIT
        ),
    )(
        in_hbm(fields),
        in_hbm(fields.reshape(V * R, C)),
        in_hbm(opacity),
        in_hbm(donor_row.reshape(1, T)),
        in_hbm(donor_column.reshape(1, T)),
        in_hbm(target_tile.reshape(1, T)),
        in_hbm(target_cell.reshape(1, T)),
        in_hbm(lagrange),
    )


def line_length(mesh):
    devices = mesh.devices[:, 0]
    spots = [getattr(device, "coords", None) for device in devices]
    if spots[0] is None:
        return len(spots)
    moved = [k for k in range(3) if len(spots) > 1 and spots[1][k] != spots[0][k]]
    if len(moved) != 1:
        return len(spots)
    count = 1
    while count < len(spots) and all(
        spots[count][k] == spots[0][k] for k in range(3) if k != moved[0]
    ):
        count += 1
    return count


def solution(mesh):
    in_specs = (
        P(None, "rad", "tile", None),
        P("rad", "tile", None),
        P("tile"),
        P("tile"),
        P("tile", None),
        P("tile"),
        P(None, "tile"),
    )
    out_specs = P(None, "rad", "tile", None)
    body = functools.partial(shards, mesh.shape["tile"], mesh.shape["rad"], line_length(mesh))
    return jax.shard_map(body, mesh=mesh, in_specs=in_specs, out_specs=out_specs, check_vma=False)
```

```python
import functools

import jax
import jax.numpy as jnp
from jax import lax
from jax.experimental import pallas as pl
from jax.experimental.pallas import tpu as pltpu
from jax.sharding import PartitionSpec as P

VISCOSITY = 0.1
COUPLING = 1.0
COOL_RATE = 2.0
TIME_STEP = 0.2
MESH = pl.DeviceIdType.MESH
LANES = 128
EVEN = lambda r: lax.rem(r, 2) == 0
ODD = lambda r: lax.rem(r, 2) == 1
ALL = lambda r: r >= 0
NONE = lambda r: r < 0
LOW = lambda r: r < 2
ZERO = lambda r: r == 0
VMEM_LIMIT = 32 << 20
STEP = 4
EARLY = 3
CROSS = 2
PRE = 3
HEAD = 0
CROSS_UP = 2
MORE = (EVEN, NONE)
FEWER = (EVEN, NONE)
SOON = 2
ORDER = (0, 1, 4, 5, 6, 2, 3, 7)
FIRST = 1
NT = (((1,), (1,)), ((), ()))


def in_hbm(x):
    return pltpu.with_memory_space_constraint(x, pltpu.HBM)


def dot(a, b):
    return jnp.dot(a, b, preferred_element_type=jnp.float32)


def split(x):
    high = x.astype(jnp.bfloat16)
    low = (x - high.astype(jnp.float32)).astype(jnp.bfloat16)
    return high, low


def pair_terms(u, ups, downs):
    s1, s2, s3 = [a + b for a, b in zip(ups, downs)]
    d1, d2, d3 = [a - b for a, b in zip(ups, downs)]
    first = (45.0 / 60.0) * d1 - (9.0 / 60.0) * d2 + (1.0 / 60.0) * d3
    second = (
        (270.0 / 180.0) * s1 - (27.0 / 180.0) * s2 + (2.0 / 180.0) * s3 - (490.0 / 180.0) * u
    )
    return first, second


def kernel(
    n_tile, n_rad, inner, cap,
    f4, f2, opacity_in, drow_in, dcol_in, ttile_in, tcell_in, lagrange_in,
    acc,
    x2, ext, taps, edge, relay, ghost, hits, chunks, inc, xall, opsum, oprecv,
    opacity, drow, dcol, ttile, tcell, lagrange,
    x2_sem, in_sem, small_sem, side_sem, turn_sem, rad_sem, far_sem, lvl_send, lvl_recv, row_send, row_recv, hop_recv, fwd_send,
    op_send, op_recv, a2a_send, a2a_recv,
):
    F, L, R, C = acc.shape
    V = F * L
    T = drow.shape[1]
    pack = LANES // cap
    VP = V // pack
    tile = lax.axis_index("tile")
    rad = lax.axis_index("rad")
    quarter = n_tile // 4
    place = lax.rem(tile, inner)
    line = tile // inner

    def each(count, visit):
        if count <= 8:
            for d in range(1, count):
                visit(d)
        else:
            lax.fori_loop(1, count, lambda d, c: (visit(d), c)[1], 0)

    halves = C // LANES
    load_x2 = [
        pltpu.make_async_copy(f2.at[:, pl.ds(h * LANES, LANES)], x2.at[h], x2_sem.at[h])
        for h in range(halves)
    ]
    load_small = [
        pltpu.make_async_copy(source, kept, small_sem.at[k])
        for k, (source, kept) in enumerate(
            [
                (dcol_in, dcol), (drow_in, drow), (lagrange_in, lagrange), (ttile_in, ttile),
                (tcell_in, tcell), (opacity_in, opacity),
            ]
        )
    ]
    load_ext = pltpu.make_async_copy(f4, ext.at[:, pl.ds(3, L)], in_sem)
    def beside(other):
        across = jnp.abs(lax.rem(other, inner) - place)
        return jnp.logical_and(
            other // inner == line, jnp.logical_or(across == 1, across == inner - 1)
        )

    def count(flag):
        return flag.astype(jnp.int32)

    side_higher = count(place < inner - 1)
    turn_higher = count(jnp.logical_and(place == inner - 1, tile < n_tile - 1))
    if inner > 2:
        side_higher = side_higher + count(place == 0)

    def signal(semaphore, to_tile, to_rad):
        pl.semaphore_signal(semaphore, inc=1, device_id=(to_tile, to_rad), device_id_type=MESH)

    barrier = pltpu.get_barrier_semaphore()

    def announce_tile(d):
        @pl.when(tile + d < n_tile)
        def _():
            signal(barrier, tile + d, rad)

    def announce_rad(d):
        @pl.when(rad + d < n_rad)
        def _():
            signal(barrier, tile, rad + d)

    each(n_tile, announce_tile)
    each(n_rad, announce_rad)


    nxt = lax.rem(tile + 1, n_tile)
    prv = lax.rem(tile + n_tile - 1, n_tile)
    has_next = jnp.logical_and(tile != quarter - 1, tile != 3 * quarter - 1)
    has_prev = jnp.logical_and(tile != quarter, tile != 3 * quarter)
    has_above = rad != n_rad - 1
    has_below = rad != 0

    half = F // 2
    relays = inner < n_tile
    order = [f for f in ORDER if f < F] if F == len(ORDER) else list(range(F))
    whole = [f for f in order if f < half or f == F - 1 or not relays]
    crosses = (place == inner - 1, place == 0)
    partner = (nxt, prv)
    via = (tile - (inner - 1), tile + (inner - 1))
    sends = (has_next, has_prev)
    origin = (lax.rem(tile + inner - 1, n_tile), lax.rem(tile + n_tile - inner + 1, n_tile))
    forwards = (
        jnp.logical_and(
            crosses[1],
            jnp.logical_and(origin[0] != quarter - 1, origin[0] != 3 * quarter - 1),
        ),
        jnp.logical_and(
            crosses[0], jnp.logical_and(origin[1] != quarter, origin[1] != 3 * quarter)
        ),
    )
    goal = (lax.rem(origin[0] + 1, n_tile), lax.rem(origin[1] + n_tile - 1, n_tile))
    strip = (pl.ds(R - 3, 3), pl.ds(0, 3))

    def row_copy(f, way):
        return pltpu.make_async_remote_copy(
            src_ref=f4.at[f, :, strip[way]], dst_ref=edge.at[f, :, strip[way]],
            send_sem=row_send.at[way], recv_sem=row_recv.at[f, way],
            device_id=(partner[way], rad), device_id_type=MESH,
        )

    def hop_copy(f, way):
        return pltpu.make_async_remote_copy(
            src_ref=f4.at[f, :, strip[way]], dst_ref=relay.at[f - shared, :, strip[way]],
            send_sem=row_send.at[way], recv_sem=hop_recv.at[f - shared, way],
            device_id=(via[way], rad), device_id_type=MESH,
        )

    def forward_copy(f, way):
        return pltpu.make_async_remote_copy(
            src_ref=relay.at[f - shared, :, strip[way]], dst_ref=edge.at[f, :, strip[way]],
            send_sem=fwd_send.at[f - shared, way], recv_sem=row_recv.at[f, way],
            device_id=(goal[way], rad), device_id_type=MESH,
        )

    shared = half - 1
    relayed = [*range(half, F), shared] if relays else []
    def by_relay(f, way, source):
        wraps = source == (n_tile - 1, 0)[way]
        if f == shared and relays:
            return jnp.logical_and(wraps, MORE[way](rad))
        if f == F - 1 and relays:
            lighter = wraps if way else jnp.logical_not(wraps)
            return jnp.logical_not(jnp.logical_and(lighter, FEWER[way](rad)))
        return jnp.logical_and(tile >= 0, f in relayed and f != shared)

    def start_hops(way):
        for f in relayed:
            through = by_relay(f, way, tile)

            @pl.when(jnp.logical_and(jnp.logical_and(sends[way], crosses[way]), through))
            def _():
                hop_copy(f, way).start()

    def start_beside(way, fields):
        for f in fields:
            @pl.when(jnp.logical_and(sends[way], jnp.logical_not(crosses[way])))
            def _():
                row_copy(f, way).start()

    def start_crossing(fields, way, ready):
        for f in fields:
            direct = jnp.logical_and(ready, jnp.logical_not(by_relay(f, way, tile)))

            @pl.when(jnp.logical_and(jnp.logical_and(sends[way], crosses[way]), direct))
            def _():
                row_copy(f, way).start()

    def forward(f):
        for way in range(2):
            @pl.when(jnp.logical_and(forwards[way], by_relay(f, way, origin[way])))
            def _():
                hop_copy(f, way).wait_recv()
                forward_copy(f, way).start()

    lvl_up = pltpu.make_async_remote_copy(
        src_ref=f4.at[:, pl.ds(L - 3, 3)], dst_ref=ext.at[:, pl.ds(0, 3)],
        send_sem=lvl_send.at[0], recv_sem=lvl_recv.at[0],
        device_id=(tile, lax.rem(rad + 1, n_rad)), device_id_type=MESH,
    )
    lvl_down = pltpu.make_async_remote_copy(
        src_ref=f4.at[:, pl.ds(0, 3)], dst_ref=ext.at[:, pl.ds(L + 3, 3)],
        send_sem=lvl_send.at[1], recv_sem=lvl_recv.at[1],
        device_id=(tile, lax.rem(rad + n_rad - 1, n_rad)), device_id_type=MESH,
    )
    op_copies = [
        pltpu.make_async_remote_copy(
            src_ref=opsum, dst_ref=oprecv.at[d - 1],
            send_sem=op_send.at[d - 1], recv_sem=op_recv.at[d - 1],
            device_id=(tile, lax.rem(rad + d, n_rad)), device_id_type=MESH,
        )
        for d in range(1, n_rad)
    ]

    def await_signals(semaphore, amount):
        @pl.when(amount > 0)
        def _():
            pl.semaphore_wait(semaphore, amount)

    await_signals(barrier, tile + rad)

    def report_tile(d):
        @pl.when(tile >= d)
        def _():
            other = tile - d

            after = jnp.logical_and(place == 0, d == 1)

            @pl.when(beside(other))
            def _():
                signal(side_sem, other, rad)

            @pl.when(after)
            def _():
                signal(turn_sem, other, rad)

            @pl.when(jnp.logical_not(jnp.logical_or(beside(other), after)))
            def _():
                signal(far_sem, other, rad)

    def report_rad(d):
        @pl.when(rad >= d)
        def _():
            signal(rad_sem, tile, rad - d)

    report_tile(1)
    start_hops(0)
    start_beside(1, order[:EARLY])
    for copy in load_small[:3] + load_x2:
        copy.start()
    start_crossing(whole[:CROSS], 0, nxt < tile)
    start_crossing(whole[:CROSS], 1, prv < tile)
    if n_tile <= 8:
        for d in range(n_tile - 1, 1, -1):
            report_tile(d)
    else:
        lax.fori_loop(2, n_tile, lambda d, c: (report_tile(d), c)[1], 0)
    each(n_rad, report_rad)

    @pl.when(has_below)
    def _():
        lvl_down.start()

    for copy in load_small[3:]:
        copy.start()
    load_ext.start()
    for copy in load_small[:3]:
        copy.wait()

    def fill_taps(span):
        diff = lax.broadcasted_iota(jnp.int32, (C, T), 0) - dcol[...]
        rows = drow[...]
        for r in span:
            weights = []
            for b in range(4):
                w = jnp.zeros((1, T), jnp.float32)
                for a in range(4):
                    w = jnp.where(rows + a == r, lagrange[4 * a + b : 4 * a + b + 1, :], w)
                weights.append(w)
            g = jnp.where(diff == 0, weights[0], 0.0)
            for b in range(1, 4):
                g = jnp.where(diff == b, weights[b], g)
            taps[0, r], taps[1, r] = split(g)

    fill_taps(range(HEAD))
    await_signals(side_sem, side_higher)
    start_hops(1)
    start_beside(0, order[:EARLY])
    fill_taps(range(HEAD, R))
    await_signals(turn_sem, turn_higher)
    start_crossing(whole[:CROSS_UP], 0, nxt > tile)
    await_signals(rad_sem, n_rad - 1 - rad)

    @pl.when(has_above)
    def _():
        lvl_up.start()

    for copy in load_x2:
        copy.wait()
    values = jnp.zeros((V, T), jnp.float32)
    for r in range(R):
        gh = taps[0, r]
        gl = taps[1, r]
        xh, xl = split(
            jnp.concatenate([x2[h, pl.ds(r, V, stride=R), :] for h in range(halves)], axis=1)
        )
        values = values + (dot(xh, gh) + (dot(xl, gh) + dot(xh, gl)))

    for copy in load_small[3:]:
        copy.wait()
    opsum[...] = jnp.sum(opacity[...], axis=0)
    target = ttile[...]
    kinds = max(16, n_tile)
    hot = (lax.broadcasted_iota(jnp.int32, (kinds, T), 0) == target).astype(jnp.float32)
    before = (
        lax.broadcasted_iota(jnp.int32, (T, T), 0) < lax.broadcasted_iota(jnp.int32, (T, T), 1)
    ).astype(jnp.float32)
    earlier = dot(hot.astype(jnp.bfloat16), before.astype(jnp.bfloat16))
    rank = jnp.sum(earlier * hot, axis=0, keepdims=True)
    key = target * cap + rank.astype(jnp.int32)
    lane_slot = lax.rem(lax.broadcasted_iota(jnp.int32, (LANES, T), 0), cap)
    vh, vl = split(values)
    label = tcell[...]
    side = lax.broadcasted_iota(jnp.int32, (16, T), 0)
    label = jnp.where(
        side == 0, label // C + 1, jnp.where(side == 1, lax.rem(label, C), 0)
    ).astype(jnp.float32).astype(jnp.bfloat16)
    stacked = jnp.concatenate([vh, vl, label], axis=0)
    lane_group = lax.broadcasted_iota(jnp.int32, (VP, LANES), 1) // cap

    def chunk(d):
        first = lax.rem(tile + d, n_tile) * cap
        chosen = (key == lane_slot + first).astype(jnp.float32).astype(jnp.bfloat16)
        moved = lax.dot_general(stacked, chosen, NT, preferred_element_type=jnp.float32)
        full = moved[:V] + moved[V : 2 * V]
        picked = full[:VP]
        for g in range(1, pack):
            picked = jnp.where(lane_group == g, full[g * VP : (g + 1) * VP], picked)
        return picked, moved[2 * V : 2 * V + 8]

    await_signals(far_sem, n_tile - 1 - tile - side_higher - turn_higher)
    start_crossing(whole[:CROSS], 1, prv > tile)
    if relays:
        for f in relayed[:SOON]:
            forward(f)

    picked, marks = chunk(0)
    inc[0, pl.ds(0, VP)] = picked
    inc[0, pl.ds(VP, 8)] = marks
    used = pl.ds(0, VP + 2)

    def a2a_copy(d):
        return pltpu.make_async_remote_copy(
            src_ref=chunks.at[d, used], dst_ref=inc.at[d, used],
            send_sem=a2a_send, recv_sem=a2a_recv.at[d],
            device_id=(lax.rem(tile + d, n_tile), rad), device_id_type=MESH,
        )

    def fill_chunk(d):
        picked, marks = chunk(d)
        chunks[d, pl.ds(0, VP)] = picked
        chunks[d, pl.ds(VP, 8)] = marks

    if n_tile <= 8:
        turns = sorted(range(1, n_tile), key=lambda d: abs(2 * d - n_tile))
        for k, d in enumerate(turns):
            fill_chunk(d)
            if k:
                a2a_copy(turns[k - 1]).start()
        a2a_copy(turns[-1]).start()
    else:
        each(n_tile, fill_chunk)
        each(n_tile, lambda d: a2a_copy(d).start())
    for copy in op_copies:
        copy.start()
    start_crossing(whole[CROSS_UP:], 0, nxt > tile)
    start_crossing(whole[CROSS:], 0, nxt < tile)
    start_crossing(whole[CROSS:], 1, tile >= 0)
    start_beside(1, order[EARLY:])
    start_beside(0, order[EARLY:])

    load_ext.wait()
    zeros3 = jnp.zeros((F, 3, R, C), jnp.float32)

    @pl.when(has_below)
    def _():
        lvl_up.wait_recv()

    @pl.when(jnp.logical_not(has_below))
    def _():
        ext[:, pl.ds(0, 3)] = zeros3

    @pl.when(has_above)
    def _():
        lvl_down.wait_recv()

    @pl.when(jnp.logical_not(has_above))
    def _():
        ext[:, pl.ds(L + 3, 3)] = zeros3

    no_rows = jnp.zeros((F, L, 3, C), jnp.float32)

    @pl.when(jnp.logical_not(has_prev))
    def _():
        edge[:, :, strip[0]] = no_rows

    @pl.when(jnp.logical_not(has_next))
    def _():
        edge[:, :, strip[1]] = no_rows

    column = lax.broadcasted_iota(jnp.int32, (STEP, R, C), 2)

    def local_part(f, i, carry):
        l = i * STEP
        u = ext[f, pl.ds(l + 3, STEP)]
        speed1 = ext[1, pl.ds(l + 3, STEP)]
        speed3 = ext[3, pl.ds(l + 3, STEP)]
        ups = [ext[f, pl.ds(l + 3 + k, STEP)] for k in (1, 2, 3)]
        downs = [ext[f, pl.ds(l + 3 - k, STEP)] for k in (1, 2, 3)]
        first, second = pair_terms(u, ups, downs)
        total = VISCOSITY * second - speed1 * first
        ups = [jnp.where(column < C - k, pltpu.roll(u, C - k, 2), 0.0) for k in (1, 2, 3)]
        downs = [jnp.where(column >= k, pltpu.roll(u, k, 2), 0.0) for k in (1, 2, 3)]
        first, second = pair_terms(u, ups, downs)
        acc[f, pl.ds(l, STEP)] = total + (VISCOSITY * second - speed3 * first)
        return carry

    for f in range(F):
        lax.fori_loop(0, L // STEP, functools.partial(local_part, f), 0)
        if f >= FIRST:
            for g in relayed[SOON + f - FIRST : SOON + f - FIRST + 1]:
                forward(g)

    above = jnp.zeros((R, C), jnp.float32)
    for d in range(1, n_rad):
        op_copies[d - 1].wait_recv()
        above = above + jnp.where(rad >= d, oprecv[d - 1], 0.0)

    def cool(l, so_far):
        mine = opacity[l]
        depth = so_far + 0.5 * mine
        acc[7, l] = acc[7, l] - COOL_RATE * jnp.exp(-depth) * ext[7, l + 3]
        return so_far + mine

    lax.fori_loop(0, L, cool, above)

    row = lax.broadcasted_iota(jnp.int32, (STEP, R, C), 1)

    def await_rows(f):
        @pl.when(has_prev)
        def _():
            row_copy(f, 0).wait_recv()

        @pl.when(has_next)
        def _():
            row_copy(f, 1).wait_recv()

    def received(f, l):
        at = pl.ds(pl.multiple_of((f * L + l) * R, STEP * R), STEP * R)
        return jnp.concatenate(
            [ghost[h, at, :].reshape(STEP, R, LANES) for h in range(halves)], axis=2
        )

    def row_part(f, finish, i, carry):
        l = i * STEP
        u = ext[f, pl.ds(l + 3, STEP)]
        speed2 = ext[2, pl.ds(l + 3, STEP)]
        rim = edge[f, pl.ds(l, STEP)]
        ups = [pltpu.roll(jnp.where(row < k, rim, u), R - k, 1) for k in (1, 2, 3)]
        downs = [pltpu.roll(jnp.where(row >= R - k, rim, u), k, 1) for k in (1, 2, 3)]
        first, second = pair_terms(u, ups, downs)
        total = acc[f, pl.ds(l, STEP)] + (VISCOSITY * second - speed2 * first)
        if finish:
            total = total + COUPLING * (received(f, l) - hits[...] * u)
            total = u + TIME_STEP * total
        acc[f, pl.ds(l, STEP)] = total
        return carry

    def ghost_part(f, i, carry):
        l = i * STEP
        u = ext[f, pl.ds(l + 3, STEP)]
        total = acc[f, pl.ds(l, STEP)] + COUPLING * (received(f, l) - hits[...] * u)
        acc[f, pl.ds(l, STEP)] = u + TIME_STEP * total
        return carry

    for f in order[:PRE]:
        await_rows(f)
        lax.fori_loop(0, L // STEP, functools.partial(row_part, f, False), 0)

    group_of = lax.broadcasted_iota(jnp.int32, (1, LANES), 1) // cap
    row_marks = {}
    column_marks = {}
    for d0 in sorted(range(0, n_tile, pack), key=lambda d: abs(2 * d + 1 - n_tile)):
        for d in range(max(d0, 1), d0 + pack):
            a2a_copy(d).wait_recv()
        lanes = pl.ds(d0 // pack * LANES, LANES)
        parts = [inc[d0 + j] for j in range(pack)]
        for g in range(pack):
            joined = None
            for j in range(pack):
                part = parts[j][:VP]
                turn = ((j - g) * cap) % LANES
                if turn:
                    part = pltpu.roll(part, turn, 1)
                joined = part if joined is None else jnp.where(lane_group == j, part, joined)
            high, low = split(joined)
            xall[pl.ds(g * VP, VP), lanes] = high
            xall[pl.ds(V + g * VP, VP), lanes] = low
        xall[pl.ds(2 * V, 16), lanes] = jnp.ones((16, LANES), jnp.bfloat16)
        row_mark = parts[0][VP : VP + 1]
        column_mark = parts[0][VP + 1 : VP + 2]
        for j in range(1, pack):
            row_mark = jnp.where(group_of == j, parts[j][VP : VP + 1], row_mark)
            column_mark = jnp.where(group_of == j, parts[j][VP + 1 : VP + 2], column_mark)
        row_marks[d0] = row_mark
        column_marks[d0] = column_mark
    row_mark = jnp.concatenate([row_marks[d] for d in sorted(row_marks)], axis=1).astype(jnp.int32)
    column_mark = jnp.concatenate([column_marks[d] for d in sorted(column_marks)], axis=1).astype(jnp.int32)
    slots = n_tile * cap
    cell_column = lax.broadcasted_iota(jnp.int32, (C, slots), 0)
    everything = xall[...]
    for r in range(R):
        wanted = jnp.where(row_mark == r + 1, column_mark, -1)
        place = (cell_column == wanted).astype(jnp.float32).astype(jnp.bfloat16)
        got = lax.dot_general(everything, place, NT, preferred_element_type=jnp.float32)
        total = got[:V] + got[V : 2 * V]
        for h in range(halves):
            ghost[h, pl.ds(r, V, stride=R), :] = total[:, h * LANES : (h + 1) * LANES]
        hits[pl.ds(r, 1), :] = got[2 * V : 2 * V + 1]


    def drain():
        @pl.when(has_above)
        def _():
            lvl_up.wait_send()

        @pl.when(has_below)
        def _():
            lvl_down.wait_send()

        for copy in op_copies:
            copy.wait_send()
        for f in relayed:
            for way in range(2):
                @pl.when(jnp.logical_and(forwards[way], by_relay(f, way, origin[way])))
                def _():
                    forward_copy(f, way).wait_send()

    def drain_rest():
        pltpu.make_async_remote_copy(
            src_ref=chunks.at[pl.ds(1, n_tile - 1), used],
            dst_ref=inc.at[pl.ds(1, n_tile - 1), used],
            send_sem=a2a_send, recv_sem=a2a_recv.at[1],
            device_id=(nxt, rad), device_id_type=MESH,
        ).wait_send()
        for way in range(2):
            @pl.when(sends[way])
            def _():
                pltpu.make_async_remote_copy(
                    src_ref=f4.at[:, :, strip[way]], dst_ref=edge.at[:, :, strip[way]],
                    send_sem=row_send.at[way], recv_sem=row_recv.at[0, way],
                    device_id=(partner[way], rad), device_id_type=MESH,
                ).wait_send()

    for f in order[:PRE]:
        lax.fori_loop(0, L // STEP, functools.partial(ghost_part, f), 0)
    for f in order[PRE:]:
        if f == order[-1]:
            drain()
        await_rows(f)
        lax.fori_loop(0, L // STEP, functools.partial(row_part, f, True), 0)

    drain_rest()


def shards(n_tile, n_rad, inner, fields, opacity, donor_row, donor_column, target_tile, target_cell, lagrange):
    F, L, R, C = fields.shape
    V = F * L
    T = donor_row.shape[0]
    cap = max(16, 2 * T // n_tile)
    pack = LANES // cap
    VP = V // pack
    hbm = pl.BlockSpec(memory_space=pltpu.HBM)
    vmem = pl.BlockSpec(memory_space=pltpu.VMEM)
    dma = pltpu.SemaphoreType.DMA
    f32 = jnp.float32
    return pl.pallas_call(
        functools.partial(kernel, n_tile, n_rad, inner, cap),
        out_shape=pltpu.VMEM(fields.shape, f32),
        in_specs=[hbm] * 8,
        out_specs=vmem,
        scratch_shapes=[
            pltpu.VMEM((C // LANES, V * R, LANES), f32),
            pltpu.VMEM((F, L + 6, R, C), f32),
            pltpu.VMEM((2, R, C, T), jnp.bfloat16),
            pltpu.VMEM((F, L, R, C), f32),
            pltpu.VMEM((F - F // 2 + 1, L, R, C), f32),
            pltpu.VMEM((C // LANES, V * R, LANES), f32),
            pltpu.VMEM((R, C), f32),
            pltpu.VMEM((n_tile, VP + 8, LANES), f32),
            pltpu.VMEM((n_tile, VP + 8, LANES), f32),
            pltpu.VMEM((2 * V + 16, n_tile * cap), jnp.bfloat16),
            pltpu.VMEM((R, C), f32),
            pltpu.VMEM((n_rad - 1, R, C), f32),
            pltpu.VMEM((L, R, C), f32),
            pltpu.VMEM((1, T), jnp.int32),
            pltpu.VMEM((1, T), jnp.int32),
            pltpu.VMEM((1, T), jnp.int32),
            pltpu.VMEM((1, T), jnp.int32),
            pltpu.VMEM(lagrange.shape, f32),
            dma((C // LANES,)),
            dma(()),
            dma((6,)),
            pltpu.SemaphoreType.REGULAR,
            pltpu.SemaphoreType.REGULAR,
            pltpu.SemaphoreType.REGULAR,
            pltpu.SemaphoreType.REGULAR,
            dma((2,)),
            dma((2,)),
            dma((2,)),
            dma((F, 2)),
            dma((F - F // 2 + 1, 2)),
            dma((F - F // 2 + 1, 2)),
            dma((n_rad - 1,)),
            dma((n_rad - 1,)),
            dma(()),
            dma((n_tile,)),
        ],
        compiler_params=pltpu.CompilerParams(
            collective_id=0, has_side_effects=True, vmem_limit_bytes=VMEM_LIMIT
        ),
    )(
        in_hbm(fields),
        in_hbm(fields.reshape(V * R, C)),
        in_hbm(opacity),
        in_hbm(donor_row.reshape(1, T)),
        in_hbm(donor_column.reshape(1, T)),
        in_hbm(target_tile.reshape(1, T)),
        in_hbm(target_cell.reshape(1, T)),
        in_hbm(lagrange),
    )


def line_length(mesh):
    devices = mesh.devices[:, 0]
    spots = [getattr(device, "coords", None) for device in devices]
    if spots[0] is None:
        return len(spots)
    moved = [k for k in range(3) if len(spots) > 1 and spots[1][k] != spots[0][k]]
    if len(moved) != 1:
        return len(spots)
    count = 1
    while count < len(spots) and all(
        spots[count][k] == spots[0][k] for k in range(3) if k != moved[0]
    ):
        count += 1
    return count


def solution(mesh):
    in_specs = (
        P(None, "rad", "tile", None),
        P("rad", "tile", None),
        P("tile"),
        P("tile"),
        P("tile", None),
        P("tile"),
        P(None, "tile"),
    )
    out_specs = P(None, "rad", "tile", None)
    body = functools.partial(shards, mesh.shape["tile"], mesh.shape["rad"], line_length(mesh))
    return jax.shard_map(body, mesh=mesh, in_specs=in_specs, out_specs=out_specs, check_vma=False)
```

```python
import functools

import jax
import jax.numpy as jnp
from jax import lax
from jax.experimental import pallas as pl
from jax.experimental.pallas import tpu as pltpu
from jax.sharding import PartitionSpec as P

VISCOSITY = 0.1
COUPLING = 1.0
COOL_RATE = 2.0
TIME_STEP = 0.2
MESH = pl.DeviceIdType.MESH
LANES = 128
EVEN = lambda r: lax.rem(r, 2) == 0
NONE = lambda r: r < 0
VMEM_LIMIT = 32 << 20
STEP = 4
EARLY = 4
CROSS = 2
PRE = 4
HEAD = 0
CROSS_UP = 2
MORE = (EVEN, NONE)
FEWER = (NONE, NONE)
SOON = 2
ORDER = (0, 1, 4, 5, 6, 2, 3, 7)
FIRST = 1
NT = (((1,), (1,)), ((), ()))
SPREAD = [TIME_STEP * VISCOSITY * w / 180.0 for w in (270.0, -27.0, 2.0)]
SLOPE = [TIME_STEP * w / 60.0 for w in (45.0, -9.0, 1.0)]


def in_hbm(x):
    return pltpu.with_memory_space_constraint(x, pltpu.HBM)


def dot(a, b):
    return jnp.dot(a, b, preferred_element_type=jnp.float32)


def split(x):
    high = x.astype(jnp.bfloat16)
    low = (x - high.astype(jnp.float32)).astype(jnp.bfloat16)
    return high, low


def pair_terms(u, ups, downs):
    s1, s2, s3 = [a + b for a, b in zip(ups, downs)]
    d1, d2, d3 = [a - b for a, b in zip(ups, downs)]
    first = (45.0 / 60.0) * d1 - (9.0 / 60.0) * d2 + (1.0 / 60.0) * d3
    second = (
        (270.0 / 180.0) * s1 - (27.0 / 180.0) * s2 + (2.0 / 180.0) * s3 - (490.0 / 180.0) * u
    )
    return first, second


def kernel(
    n_tile, n_rad, inner, cap,
    f4, f2, opacity_in, drow_in, dcol_in, ttile_in, tcell_in, lagrange_in,
    acc,
    x2, ext, taps, edge, relay, ghost, hits, chunks, inc, xall, opsum, oprecv,
    opacity, drow, dcol, ttile, tcell, lagrange,
    x2_sem, in_sem, small_sem, side_sem, turn_sem, rad_sem, far_sem, lvl_send, lvl_recv, row_send, row_recv, hop_recv, fwd_send,
    op_send, op_recv, a2a_send, a2a_recv,
):
    F, L, R, C = acc.shape
    V = F * L
    T = drow.shape[1]
    pack = LANES // cap
    VP = V // pack
    tile = lax.axis_index("tile")
    rad = lax.axis_index("rad")
    quarter = n_tile // 4
    place = lax.rem(tile, inner)
    line = tile // inner

    def each(count, visit):
        if count <= 8:
            for d in range(1, count):
                visit(d)
        else:
            lax.fori_loop(1, count, lambda d, c: (visit(d), c)[1], 0)

    halves = C // LANES
    load_x2 = [
        pltpu.make_async_copy(f2.at[:, pl.ds(h * LANES, LANES)], x2.at[h], x2_sem.at[h])
        for h in range(halves)
    ]
    load_small = [
        pltpu.make_async_copy(source, kept, small_sem.at[k])
        for k, (source, kept) in enumerate(
            [
                (dcol_in, dcol), (drow_in, drow), (lagrange_in, lagrange), (ttile_in, ttile),
                (tcell_in, tcell), (opacity_in, opacity),
            ]
        )
    ]
    load_ext = pltpu.make_async_copy(f4, ext.at[:, pl.ds(3, L)], in_sem)
    def beside(other):
        across = jnp.abs(lax.rem(other, inner) - place)
        return jnp.logical_and(
            other // inner == line, jnp.logical_or(across == 1, across == inner - 1)
        )

    def count(flag):
        return flag.astype(jnp.int32)

    side_higher = count(place < inner - 1)
    turn_higher = count(jnp.logical_and(place == inner - 1, tile < n_tile - 1))
    if inner > 2:
        side_higher = side_higher + count(place == 0)

    def signal(semaphore, to_tile, to_rad):
        pl.semaphore_signal(semaphore, inc=1, device_id=(to_tile, to_rad), device_id_type=MESH)

    barrier = pltpu.get_barrier_semaphore()

    def announce_tile(d):
        @pl.when(tile + d < n_tile)
        def _():
            signal(barrier, tile + d, rad)

    def announce_rad(d):
        @pl.when(rad + d < n_rad)
        def _():
            signal(barrier, tile, rad + d)

    each(n_tile, announce_tile)
    each(n_rad, announce_rad)


    nxt = lax.rem(tile + 1, n_tile)
    prv = lax.rem(tile + n_tile - 1, n_tile)
    has_next = jnp.logical_and(tile != quarter - 1, tile != 3 * quarter - 1)
    has_prev = jnp.logical_and(tile != quarter, tile != 3 * quarter)
    has_above = rad != n_rad - 1
    has_below = rad != 0

    half = F // 2
    relays = inner < n_tile
    order = [f for f in ORDER if f < F] if F == len(ORDER) else list(range(F))
    whole = [f for f in order if f < half or f == F - 1 or not relays]
    crosses = (place == inner - 1, place == 0)
    partner = (nxt, prv)
    via = (tile - (inner - 1), tile + (inner - 1))
    sends = (has_next, has_prev)
    origin = (lax.rem(tile + inner - 1, n_tile), lax.rem(tile + n_tile - inner + 1, n_tile))
    forwards = (
        jnp.logical_and(
            crosses[1],
            jnp.logical_and(origin[0] != quarter - 1, origin[0] != 3 * quarter - 1),
        ),
        jnp.logical_and(
            crosses[0], jnp.logical_and(origin[1] != quarter, origin[1] != 3 * quarter)
        ),
    )
    goal = (lax.rem(origin[0] + 1, n_tile), lax.rem(origin[1] + n_tile - 1, n_tile))
    strip = (pl.ds(R - 3, 3), pl.ds(0, 3))

    def row_copy(f, way):
        return pltpu.make_async_remote_copy(
            src_ref=f4.at[f, :, strip[way]], dst_ref=edge.at[f, :, strip[way]],
            send_sem=row_send.at[way], recv_sem=row_recv.at[f, way],
            device_id=(partner[way], rad), device_id_type=MESH,
        )

    def hop_copy(f, way):
        return pltpu.make_async_remote_copy(
            src_ref=f4.at[f, :, strip[way]], dst_ref=relay.at[f - shared, :, strip[way]],
            send_sem=row_send.at[way], recv_sem=hop_recv.at[f - shared, way],
            device_id=(via[way], rad), device_id_type=MESH,
        )

    def forward_copy(f, way):
        return pltpu.make_async_remote_copy(
            src_ref=relay.at[f - shared, :, strip[way]], dst_ref=edge.at[f, :, strip[way]],
            send_sem=fwd_send.at[f - shared, way], recv_sem=row_recv.at[f, way],
            device_id=(goal[way], rad), device_id_type=MESH,
        )

    shared = half - 1
    relayed = [*range(half, F), shared] if relays else []
    def by_relay(f, way, source):
        wraps = source == (n_tile - 1, 0)[way]
        if f == shared and relays:
            return jnp.logical_and(wraps, MORE[way](rad))
        if f == F - 1 and relays:
            lighter = wraps if way else jnp.logical_not(wraps)
            return jnp.logical_not(jnp.logical_and(lighter, FEWER[way](rad)))
        return jnp.logical_and(tile >= 0, f in relayed and f != shared)

    def start_hops(way):
        for f in relayed:
            through = by_relay(f, way, tile)

            @pl.when(jnp.logical_and(jnp.logical_and(sends[way], crosses[way]), through))
            def _():
                hop_copy(f, way).start()

    def start_beside(way, fields):
        for f in fields:
            @pl.when(jnp.logical_and(sends[way], jnp.logical_not(crosses[way])))
            def _():
                row_copy(f, way).start()

    def start_crossing(fields, way, ready):
        for f in fields:
            direct = jnp.logical_and(ready, jnp.logical_not(by_relay(f, way, tile)))

            @pl.when(jnp.logical_and(jnp.logical_and(sends[way], crosses[way]), direct))
            def _():
                row_copy(f, way).start()

    def forward(f):
        for way in range(2):
            @pl.when(jnp.logical_and(forwards[way], by_relay(f, way, origin[way])))
            def _():
                hop_copy(f, way).wait_recv()
                forward_copy(f, way).start()

    lvl_up = pltpu.make_async_remote_copy(
        src_ref=f4.at[:, pl.ds(L - 3, 3)], dst_ref=ext.at[:, pl.ds(0, 3)],
        send_sem=lvl_send.at[0], recv_sem=lvl_recv.at[0],
        device_id=(tile, lax.rem(rad + 1, n_rad)), device_id_type=MESH,
    )
    lvl_down = pltpu.make_async_remote_copy(
        src_ref=f4.at[:, pl.ds(0, 3)], dst_ref=ext.at[:, pl.ds(L + 3, 3)],
        send_sem=lvl_send.at[1], recv_sem=lvl_recv.at[1],
        device_id=(tile, lax.rem(rad + n_rad - 1, n_rad)), device_id_type=MESH,
    )
    op_copies = [
        pltpu.make_async_remote_copy(
            src_ref=opsum, dst_ref=oprecv.at[d - 1],
            send_sem=op_send.at[d - 1], recv_sem=op_recv.at[d - 1],
            device_id=(tile, lax.rem(rad + d, n_rad)), device_id_type=MESH,
        )
        for d in range(1, n_rad)
    ]

    def await_signals(semaphore, amount):
        @pl.when(amount > 0)
        def _():
            pl.semaphore_wait(semaphore, amount)

    await_signals(barrier, tile + rad)

    def report_tile(d):
        @pl.when(tile >= d)
        def _():
            other = tile - d

            after = jnp.logical_and(place == 0, d == 1)

            @pl.when(beside(other))
            def _():
                signal(side_sem, other, rad)

            @pl.when(after)
            def _():
                signal(turn_sem, other, rad)

            @pl.when(jnp.logical_not(jnp.logical_or(beside(other), after)))
            def _():
                signal(far_sem, other, rad)

    def report_rad(d):
        @pl.when(rad >= d)
        def _():
            signal(rad_sem, tile, rad - d)

    report_tile(1)
    start_hops(0)
    start_beside(1, order[:EARLY])
    for copy in load_small[:3] + load_x2:
        copy.start()
    start_crossing(whole[:CROSS], 0, nxt < tile)
    start_crossing(whole[:CROSS], 1, prv < tile)
    if n_tile <= 8:
        for d in range(n_tile - 1, 1, -1):
            report_tile(d)
    else:
        lax.fori_loop(2, n_tile, lambda d, c: (report_tile(d), c)[1], 0)
    each(n_rad, report_rad)

    @pl.when(has_below)
    def _():
        lvl_down.start()

    for copy in load_small[3:]:
        copy.start()
    load_ext.start()
    for copy in load_small[:3]:
        copy.wait()

    def fill_taps(span):
        diff = lax.broadcasted_iota(jnp.int32, (C, T), 0) - dcol[...]
        rows = drow[...]
        for r in span:
            weights = []
            for b in range(4):
                w = jnp.zeros((1, T), jnp.float32)
                for a in range(4):
                    w = jnp.where(rows + a == r, lagrange[4 * a + b : 4 * a + b + 1, :], w)
                weights.append(w)
            g = jnp.where(diff == 0, weights[0], 0.0)
            for b in range(1, 4):
                g = jnp.where(diff == b, weights[b], g)
            taps[0, r], taps[1, r] = split(g)

    fill_taps(range(HEAD))
    await_signals(side_sem, side_higher)
    start_hops(1)
    start_beside(0, order[:EARLY])
    fill_taps(range(HEAD, R))
    await_signals(turn_sem, turn_higher)
    start_crossing(whole[:CROSS_UP], 0, nxt > tile)
    await_signals(rad_sem, n_rad - 1 - rad)

    @pl.when(has_above)
    def _():
        lvl_up.start()

    for copy in load_x2:
        copy.wait()
    values = jnp.zeros((V, T), jnp.float32)
    for r in range(R):
        gh = taps[0, r]
        gl = taps[1, r]
        xh, xl = split(
            jnp.concatenate([x2[h, pl.ds(r, V, stride=R), :] for h in range(halves)], axis=1)
        )
        values = values + (dot(xh, gh) + (dot(xl, gh) + dot(xh, gl)))

    for copy in load_small[3:]:
        copy.wait()
    target = ttile[...]
    kinds = max(16, n_tile)
    hot = (lax.broadcasted_iota(jnp.int32, (kinds, T), 0) == target).astype(jnp.float32)
    before = (
        lax.broadcasted_iota(jnp.int32, (T, T), 0) < lax.broadcasted_iota(jnp.int32, (T, T), 1)
    ).astype(jnp.float32)
    earlier = dot(hot.astype(jnp.bfloat16), before.astype(jnp.bfloat16))
    rank = jnp.sum(earlier * hot, axis=0, keepdims=True)
    key = target * cap + rank.astype(jnp.int32)
    lane_slot = lax.rem(lax.broadcasted_iota(jnp.int32, (LANES, T), 0), cap)
    vh, vl = split(values)
    label = tcell[...]
    side = lax.broadcasted_iota(jnp.int32, (16, T), 0)
    label = jnp.where(
        side == 0, label // C + 1, jnp.where(side == 1, lax.rem(label, C), 0)
    ).astype(jnp.float32).astype(jnp.bfloat16)
    stacked = jnp.concatenate([vh, vl, label], axis=0)
    lane_group = lax.broadcasted_iota(jnp.int32, (VP, LANES), 1) // cap

    def chunk(d):
        first = lax.rem(tile + d, n_tile) * cap
        chosen = (key == lane_slot + first).astype(jnp.float32).astype(jnp.bfloat16)
        moved = lax.dot_general(stacked, chosen, NT, preferred_element_type=jnp.float32)
        full = moved[:V] + moved[V : 2 * V]
        picked = full[:VP]
        for g in range(1, pack):
            picked = jnp.where(lane_group == g, full[g * VP : (g + 1) * VP], picked)
        return picked, moved[2 * V : 2 * V + 8]

    await_signals(far_sem, n_tile - 1 - tile - side_higher - turn_higher)
    start_crossing(whole[:CROSS], 1, prv > tile)
    if relays:
        for f in relayed[:SOON]:
            forward(f)

    used = pl.ds(0, VP + 2)

    def a2a_copy(d):
        return pltpu.make_async_remote_copy(
            src_ref=chunks.at[d, used], dst_ref=inc.at[d, used],
            send_sem=a2a_send, recv_sem=a2a_recv.at[d],
            device_id=(lax.rem(tile + d, n_tile), rad), device_id_type=MESH,
        )

    def fill_chunk(d):
        picked, marks = chunk(d)
        chunks[d, pl.ds(0, VP)] = picked
        chunks[d, pl.ds(VP, 8)] = marks

    if n_tile <= 8:
        turns = sorted(range(1, n_tile), key=lambda d: abs(2 * d - n_tile))
        for k, d in enumerate(turns):
            fill_chunk(d)
            if k:
                a2a_copy(turns[k - 1]).start()
        a2a_copy(turns[-1]).start()
    else:
        each(n_tile, fill_chunk)
        each(n_tile, lambda d: a2a_copy(d).start())
    opsum[...] = jnp.sum(opacity[...], axis=0)
    start_crossing(whole[CROSS_UP:], 0, nxt > tile)
    start_crossing(whole[CROSS:], 0, nxt < tile)
    start_crossing(whole[CROSS:], 1, tile >= 0)
    start_beside(1, order[EARLY:])
    start_beside(0, order[EARLY:])
    picked, marks = chunk(0)
    inc[0, pl.ds(0, VP)] = picked
    inc[0, pl.ds(VP, 8)] = marks
    for copy in op_copies:
        copy.start()

    load_ext.wait()
    zeros3 = jnp.zeros((F, 3, R, C), jnp.float32)

    @pl.when(has_below)
    def _():
        lvl_up.wait_recv()

    @pl.when(jnp.logical_not(has_below))
    def _():
        ext[:, pl.ds(0, 3)] = zeros3

    @pl.when(has_above)
    def _():
        lvl_down.wait_recv()

    @pl.when(jnp.logical_not(has_above))
    def _():
        ext[:, pl.ds(L + 3, 3)] = zeros3

    no_rows = jnp.zeros((F, L, 3, C), jnp.float32)

    @pl.when(jnp.logical_not(has_prev))
    def _():
        edge[:, :, strip[0]] = no_rows

    @pl.when(jnp.logical_not(has_next))
    def _():
        edge[:, :, strip[1]] = no_rows

    column = lax.broadcasted_iota(jnp.int32, (STEP, R, C), 2)

    def local_part(f, i, carry):
        l = i * STEP
        u = ext[f, pl.ds(l + 3, STEP)]
        speed1 = ext[1, pl.ds(l + 3, STEP)]
        speed3 = ext[3, pl.ds(l + 3, STEP)]
        ups = [ext[f, pl.ds(l + 3 + k, STEP)] for k in (1, 2, 3)]
        downs = [ext[f, pl.ds(l + 3 - k, STEP)] for k in (1, 2, 3)]
        first, second = pair_terms(u, ups, downs)
        total = VISCOSITY * second - speed1 * first
        ups = [jnp.where(column < C - k, pltpu.roll(u, C - k, 2), 0.0) for k in (1, 2, 3)]
        downs = [jnp.where(column >= k, pltpu.roll(u, k, 2), 0.0) for k in (1, 2, 3)]
        first, second = pair_terms(u, ups, downs)
        acc[f, pl.ds(l, STEP)] = total + (VISCOSITY * second - speed3 * first)
        return carry

    for f in range(F):
        lax.fori_loop(0, L // STEP, functools.partial(local_part, f), 0)
        if f >= FIRST:
            for g in relayed[SOON + f - FIRST : SOON + f - FIRST + 1]:
                forward(g)

    above = jnp.zeros((R, C), jnp.float32)
    for d in range(1, n_rad):
        op_copies[d - 1].wait_recv()
        above = above + jnp.where(rad >= d, oprecv[d - 1], 0.0)

    def cool(l, so_far):
        mine = opacity[l]
        depth = so_far + 0.5 * mine
        acc[7, l] = acc[7, l] - COOL_RATE * jnp.exp(-depth) * ext[7, l + 3]
        return so_far + mine

    lax.fori_loop(0, L, cool, above)

    row = lax.broadcasted_iota(jnp.int32, (STEP, R, C), 1)

    def await_rows(f):
        @pl.when(has_prev)
        def _():
            row_copy(f, 0).wait_recv()

        @pl.when(has_next)
        def _():
            row_copy(f, 1).wait_recv()

    def received(f, l):
        at = pl.ds(pl.multiple_of((f * L + l) * R, STEP * R), STEP * R)
        return jnp.concatenate(
            [ghost[h, at, :].reshape(STEP, R, LANES) for h in range(halves)], axis=2
        )

    def row_part(f, keep, i, carry):
        l = i * STEP
        u = ext[f, pl.ds(l + 3, STEP)]
        speed2 = ext[2, pl.ds(l + 3, STEP)]
        rim = edge[f, pl.ds(l, STEP)]
        ups = [pltpu.roll(jnp.where(row < k, rim, u), R - k, 1) for k in (1, 2, 3)]
        downs = [pltpu.roll(jnp.where(row >= R - k, rim, u), k, 1) for k in (1, 2, 3)]
        if keep is not None:
            sums = [a + b for a, b in zip(ups, downs)]
            jumps = [a - b for a, b in zip(ups, downs)]
            spread = sum(w * a for w, a in zip(SPREAD, sums))
            slope = sum(w * a for w, a in zip(SLOPE, jumps))
            total = TIME_STEP * (acc[f, pl.ds(l, STEP)] + COUPLING * received(f, l))
            total = total + keep * u + (spread - speed2 * slope)
        else:
            first, second = pair_terms(u, ups, downs)
            total = acc[f, pl.ds(l, STEP)] + (VISCOSITY * second - speed2 * first)
        acc[f, pl.ds(l, STEP)] = total
        return carry

    def ghost_part(f, i, carry):
        l = i * STEP
        u = ext[f, pl.ds(l + 3, STEP)]
        total = acc[f, pl.ds(l, STEP)] + COUPLING * (received(f, l) - hits[...] * u)
        acc[f, pl.ds(l, STEP)] = u + TIME_STEP * total
        return carry

    for f in order[:PRE]:
        await_rows(f)
        lax.fori_loop(0, L // STEP, functools.partial(row_part, f, None), 0)

    group_of = lax.broadcasted_iota(jnp.int32, (1, LANES), 1) // cap
    row_marks = {}
    column_marks = {}
    for d0 in sorted(range(0, n_tile, pack), key=lambda d: abs(2 * d + 1 - n_tile)):
        for d in range(max(d0, 1), d0 + pack):
            a2a_copy(d).wait_recv()
        lanes = pl.ds(d0 // pack * LANES, LANES)
        parts = [inc[d0 + j] for j in range(pack)]
        for g in range(pack):
            joined = None
            for j in range(pack):
                part = parts[j][:VP]
                turn = ((j - g) * cap) % LANES
                if turn:
                    part = pltpu.roll(part, turn, 1)
                joined = part if joined is None else jnp.where(lane_group == j, part, joined)
            high, low = split(joined)
            xall[pl.ds(g * VP, VP), lanes] = high
            xall[pl.ds(V + g * VP, VP), lanes] = low
        xall[pl.ds(2 * V, 16), lanes] = jnp.ones((16, LANES), jnp.bfloat16)
        row_mark = parts[0][VP : VP + 1]
        column_mark = parts[0][VP + 1 : VP + 2]
        for j in range(1, pack):
            row_mark = jnp.where(group_of == j, parts[j][VP : VP + 1], row_mark)
            column_mark = jnp.where(group_of == j, parts[j][VP + 1 : VP + 2], column_mark)
        row_marks[d0] = row_mark
        column_marks[d0] = column_mark
    row_mark = jnp.concatenate([row_marks[d] for d in sorted(row_marks)], axis=1).astype(jnp.int32)
    column_mark = jnp.concatenate([column_marks[d] for d in sorted(column_marks)], axis=1).astype(jnp.int32)
    slots = n_tile * cap
    cell_column = lax.broadcasted_iota(jnp.int32, (C, slots), 0)
    everything = xall[...]
    for r in range(R):
        wanted = jnp.where(row_mark == r + 1, column_mark, -1)
        place = (cell_column == wanted).astype(jnp.float32).astype(jnp.bfloat16)
        got = lax.dot_general(everything, place, NT, preferred_element_type=jnp.float32)
        total = got[:V] + got[V : 2 * V]
        for h in range(halves):
            ghost[h, pl.ds(r, V, stride=R), :] = total[:, h * LANES : (h + 1) * LANES]
        hits[pl.ds(r, 1), :] = got[2 * V : 2 * V + 1]


    def drain():
        @pl.when(has_above)
        def _():
            lvl_up.wait_send()

        @pl.when(has_below)
        def _():
            lvl_down.wait_send()

        for copy in op_copies:
            copy.wait_send()
        for f in relayed:
            for way in range(2):
                @pl.when(jnp.logical_and(forwards[way], by_relay(f, way, origin[way])))
                def _():
                    forward_copy(f, way).wait_send()

    def drain_rest():
        pltpu.make_async_remote_copy(
            src_ref=chunks.at[pl.ds(1, n_tile - 1), used],
            dst_ref=inc.at[pl.ds(1, n_tile - 1), used],
            send_sem=a2a_send, recv_sem=a2a_recv.at[1],
            device_id=(nxt, rad), device_id_type=MESH,
        ).wait_send()
        for way in range(2):
            @pl.when(sends[way])
            def _():
                pltpu.make_async_remote_copy(
                    src_ref=f4.at[:, :, strip[way]], dst_ref=edge.at[:, :, strip[way]],
                    send_sem=row_send.at[way], recv_sem=row_recv.at[0, way],
                    device_id=(partner[way], rad), device_id_type=MESH,
                ).wait_send()

    for f in order[:PRE]:
        lax.fori_loop(0, L // STEP, functools.partial(ghost_part, f), 0)
    keep = (1.0 + TIME_STEP * VISCOSITY * (-490.0 / 180.0)) - TIME_STEP * COUPLING * hits[...]
    for f in order[PRE:]:
        if f == order[-1]:
            drain()
        await_rows(f)
        lax.fori_loop(0, L // STEP, functools.partial(row_part, f, keep), 0)

    drain_rest()


def shards(n_tile, n_rad, inner, fields, opacity, donor_row, donor_column, target_tile, target_cell, lagrange):
    F, L, R, C = fields.shape
    V = F * L
    T = donor_row.shape[0]
    cap = max(16, 2 * T // n_tile)
    pack = LANES // cap
    VP = V // pack
    hbm = pl.BlockSpec(memory_space=pltpu.HBM)
    vmem = pl.BlockSpec(memory_space=pltpu.VMEM)
    dma = pltpu.SemaphoreType.DMA
    f32 = jnp.float32
    return pl.pallas_call(
        functools.partial(kernel, n_tile, n_rad, inner, cap),
        out_shape=pltpu.VMEM(fields.shape, f32),
        in_specs=[hbm] * 8,
        out_specs=vmem,
        scratch_shapes=[
            pltpu.VMEM((C // LANES, V * R, LANES), f32),
            pltpu.VMEM((F, L + 6, R, C), f32),
            pltpu.VMEM((2, R, C, T), jnp.bfloat16),
            pltpu.VMEM((F, L, R, C), f32),
            pltpu.VMEM((F - F // 2 + 1, L, R, C), f32),
            pltpu.VMEM((C // LANES, V * R, LANES), f32),
            pltpu.VMEM((R, C), f32),
            pltpu.VMEM((n_tile, VP + 8, LANES), f32),
            pltpu.VMEM((n_tile, VP + 8, LANES), f32),
            pltpu.VMEM((2 * V + 16, n_tile * cap), jnp.bfloat16),
            pltpu.VMEM((R, C), f32),
            pltpu.VMEM((n_rad - 1, R, C), f32),
            pltpu.VMEM((L, R, C), f32),
            pltpu.VMEM((1, T), jnp.int32),
            pltpu.VMEM((1, T), jnp.int32),
            pltpu.VMEM((1, T), jnp.int32),
            pltpu.VMEM((1, T), jnp.int32),
            pltpu.VMEM(lagrange.shape, f32),
            dma((C // LANES,)),
            dma(()),
            dma((6,)),
            pltpu.SemaphoreType.REGULAR,
            pltpu.SemaphoreType.REGULAR,
            pltpu.SemaphoreType.REGULAR,
            pltpu.SemaphoreType.REGULAR,
            dma((2,)),
            dma((2,)),
            dma((2,)),
            dma((F, 2)),
            dma((F - F // 2 + 1, 2)),
            dma((F - F // 2 + 1, 2)),
            dma((n_rad - 1,)),
            dma((n_rad - 1,)),
            dma(()),
            dma((n_tile,)),
        ],
        compiler_params=pltpu.CompilerParams(
            collective_id=0, has_side_effects=True, vmem_limit_bytes=VMEM_LIMIT
        ),
    )(
        in_hbm(fields),
        in_hbm(fields.reshape(V * R, C)),
        in_hbm(opacity),
        in_hbm(donor_row.reshape(1, T)),
        in_hbm(donor_column.reshape(1, T)),
        in_hbm(target_tile.reshape(1, T)),
        in_hbm(target_cell.reshape(1, T)),
        in_hbm(lagrange),
    )


def line_length(mesh):
    devices = mesh.devices[:, 0]
    spots = [getattr(device, "coords", None) for device in devices]
    if spots[0] is None:
        return len(spots)
    moved = [k for k in range(3) if len(spots) > 1 and spots[1][k] != spots[0][k]]
    if len(moved) != 1:
        return len(spots)
    count = 1
    while count < len(spots) and all(
        spots[count][k] == spots[0][k] for k in range(3) if k != moved[0]
    ):
        count += 1
    return count


def solution(mesh):
    in_specs = (
        P(None, "rad", "tile", None),
        P("rad", "tile", None),
        P("tile"),
        P("tile"),
        P("tile", None),
        P("tile"),
        P(None, "tile"),
    )
    out_specs = P(None, "rad", "tile", None)
    body = functools.partial(shards, mesh.shape["tile"], mesh.shape["rad"], line_length(mesh))
    return jax.shard_map(body, mesh=mesh, in_specs=in_specs, out_specs=out_specs, check_vma=False)
```

```python
import functools

import jax
import jax.numpy as jnp
from jax import lax
from jax.experimental import pallas as pl
from jax.experimental.pallas import tpu as pltpu
from jax.sharding import PartitionSpec as P

VISCOSITY = 0.1
COUPLING = 1.0
COOL_RATE = 2.0
TIME_STEP = 0.2
MESH = pl.DeviceIdType.MESH
LANES = 128
EVEN = lambda r: lax.rem(r, 2) == 0
NONE = lambda r: r < 0
VMEM_LIMIT = 32 << 20
STEP = 8
EARLY = 4
CROSS = 2
PRE = 4
HEAD = 0
CROSS_UP = 2
MORE = (EVEN, NONE)
FEWER = (NONE, NONE)
SOON = 2
ORDER = (0, 1, 4, 5, 6, 2, 3, 7)
FIRST = 0
NT = (((1,), (1,)), ((), ()))
SPREAD = [TIME_STEP * VISCOSITY * w / 180.0 for w in (270.0, -27.0, 2.0)]
SLOPE = [TIME_STEP * w / 60.0 for w in (45.0, -9.0, 1.0)]


def in_hbm(x):
    return pltpu.with_memory_space_constraint(x, pltpu.HBM)


def dot(a, b):
    return jnp.dot(a, b, preferred_element_type=jnp.float32)


def split(x):
    high = x.astype(jnp.bfloat16)
    low = (x - high.astype(jnp.float32)).astype(jnp.bfloat16)
    return high, low


def pair_terms(u, ups, downs):
    s1, s2, s3 = [a + b for a, b in zip(ups, downs)]
    d1, d2, d3 = [a - b for a, b in zip(ups, downs)]
    first = (45.0 / 60.0) * d1 - (9.0 / 60.0) * d2 + (1.0 / 60.0) * d3
    second = (
        (270.0 / 180.0) * s1 - (27.0 / 180.0) * s2 + (2.0 / 180.0) * s3 - (490.0 / 180.0) * u
    )
    return first, second


def kernel(
    n_tile, n_rad, inner, cap,
    f4, f2, opacity_in, drow_in, dcol_in, ttile_in, tcell_in, lagrange_in,
    acc,
    x2, ext, taps, edge, relay, ghost, hits, chunks, inc, xall, opsum, oprecv,
    opacity, drow, dcol, ttile, tcell, lagrange,
    x2_sem, in_sem, small_sem, side_sem, turn_sem, rad_sem, far_sem, lvl_send, lvl_recv, row_send, row_recv, hop_recv, fwd_send,
    op_send, op_recv, a2a_send, a2a_recv,
):
    F, L, R, C = acc.shape
    V = F * L
    T = drow.shape[1]
    pack = LANES // cap
    VP = V // pack
    tile = lax.axis_index("tile")
    rad = lax.axis_index("rad")
    quarter = n_tile // 4
    place = lax.rem(tile, inner)
    line = tile // inner

    def each(count, visit):
        if count <= 8:
            for d in range(1, count):
                visit(d)
        else:
            lax.fori_loop(1, count, lambda d, c: (visit(d), c)[1], 0)

    halves = C // LANES
    load_x2 = [
        pltpu.make_async_copy(f2.at[:, pl.ds(h * LANES, LANES)], x2.at[h], x2_sem.at[h])
        for h in range(halves)
    ]
    load_small = [
        pltpu.make_async_copy(source, kept, small_sem.at[k])
        for k, (source, kept) in enumerate(
            [
                (dcol_in, dcol), (drow_in, drow), (lagrange_in, lagrange), (ttile_in, ttile),
                (tcell_in, tcell), (opacity_in, opacity),
            ]
        )
    ]
    load_ext = pltpu.make_async_copy(f4, ext.at[:, pl.ds(3, L)], in_sem)
    def beside(other):
        across = jnp.abs(lax.rem(other, inner) - place)
        return jnp.logical_and(
            other // inner == line, jnp.logical_or(across == 1, across == inner - 1)
        )

    def count(flag):
        return flag.astype(jnp.int32)

    side_higher = count(place < inner - 1)
    turn_higher = count(jnp.logical_and(place == inner - 1, tile < n_tile - 1))
    if inner > 2:
        side_higher = side_higher + count(place == 0)

    def signal(semaphore, to_tile, to_rad):
        pl.semaphore_signal(semaphore, inc=1, device_id=(to_tile, to_rad), device_id_type=MESH)

    barrier = pltpu.get_barrier_semaphore()

    def announce_tile(d):
        @pl.when(tile + d < n_tile)
        def _():
            signal(barrier, tile + d, rad)

    def announce_rad(d):
        @pl.when(rad + d < n_rad)
        def _():
            signal(barrier, tile, rad + d)

    each(n_tile, announce_tile)
    each(n_rad, announce_rad)


    nxt = lax.rem(tile + 1, n_tile)
    prv = lax.rem(tile + n_tile - 1, n_tile)
    has_next = jnp.logical_and(tile != quarter - 1, tile != 3 * quarter - 1)
    has_prev = jnp.logical_and(tile != quarter, tile != 3 * quarter)
    has_above = rad != n_rad - 1
    has_below = rad != 0

    half = F // 2
    relays = inner < n_tile
    order = [f for f in ORDER if f < F] if F == len(ORDER) else list(range(F))
    whole = [f for f in order if f < half or f == F - 1 or not relays]
    crosses = (place == inner - 1, place == 0)
    partner = (nxt, prv)
    via = (tile - (inner - 1), tile + (inner - 1))
    sends = (has_next, has_prev)
    origin = (lax.rem(tile + inner - 1, n_tile), lax.rem(tile + n_tile - inner + 1, n_tile))
    forwards = (
        jnp.logical_and(
            crosses[1],
            jnp.logical_and(origin[0] != quarter - 1, origin[0] != 3 * quarter - 1),
        ),
        jnp.logical_and(
            crosses[0], jnp.logical_and(origin[1] != quarter, origin[1] != 3 * quarter)
        ),
    )
    goal = (lax.rem(origin[0] + 1, n_tile), lax.rem(origin[1] + n_tile - 1, n_tile))
    strip = (pl.ds(R - 3, 3), pl.ds(0, 3))

    def row_copy(f, way):
        return pltpu.make_async_remote_copy(
            src_ref=f4.at[f, :, strip[way]], dst_ref=edge.at[f, :, strip[way]],
            send_sem=row_send.at[way], recv_sem=row_recv.at[f, way],
            device_id=(partner[way], rad), device_id_type=MESH,
        )

    def hop_copy(f, way):
        return pltpu.make_async_remote_copy(
            src_ref=f4.at[f, :, strip[way]], dst_ref=relay.at[f - shared, :, strip[way]],
            send_sem=row_send.at[way], recv_sem=hop_recv.at[f - shared, way],
            device_id=(via[way], rad), device_id_type=MESH,
        )

    def forward_copy(f, way):
        return pltpu.make_async_remote_copy(
            src_ref=relay.at[f - shared, :, strip[way]], dst_ref=edge.at[f, :, strip[way]],
            send_sem=fwd_send.at[f - shared, way], recv_sem=row_recv.at[f, way],
            device_id=(goal[way], rad), device_id_type=MESH,
        )

    shared = half - 1
    relayed = [*range(half, F), shared] if relays else []
    def by_relay(f, way, source):
        wraps = source == (n_tile - 1, 0)[way]
        if f == shared and relays:
            return jnp.logical_and(wraps, MORE[way](rad))
        if f == F - 1 and relays:
            lighter = wraps if way else jnp.logical_not(wraps)
            return jnp.logical_not(jnp.logical_and(lighter, FEWER[way](rad)))
        return jnp.logical_and(tile >= 0, f in relayed and f != shared)

    def start_hops(way):
        for f in relayed:
            through = by_relay(f, way, tile)

            @pl.when(jnp.logical_and(jnp.logical_and(sends[way], crosses[way]), through))
            def _():
                hop_copy(f, way).start()

    def start_beside(way, fields):
        for f in fields:
            @pl.when(jnp.logical_and(sends[way], jnp.logical_not(crosses[way])))
            def _():
                row_copy(f, way).start()

    def start_crossing(fields, way, ready):
        for f in fields:
            direct = jnp.logical_and(ready, jnp.logical_not(by_relay(f, way, tile)))

            @pl.when(jnp.logical_and(jnp.logical_and(sends[way], crosses[way]), direct))
            def _():
                row_copy(f, way).start()

    def forward(f):
        for way in range(2):
            @pl.when(jnp.logical_and(forwards[way], by_relay(f, way, origin[way])))
            def _():
                hop_copy(f, way).wait_recv()
                forward_copy(f, way).start()

    lvl_up = pltpu.make_async_remote_copy(
        src_ref=f4.at[:, pl.ds(L - 3, 3)], dst_ref=ext.at[:, pl.ds(0, 3)],
        send_sem=lvl_send.at[0], recv_sem=lvl_recv.at[0],
        device_id=(tile, lax.rem(rad + 1, n_rad)), device_id_type=MESH,
    )
    lvl_down = pltpu.make_async_remote_copy(
        src_ref=f4.at[:, pl.ds(0, 3)], dst_ref=ext.at[:, pl.ds(L + 3, 3)],
        send_sem=lvl_send.at[1], recv_sem=lvl_recv.at[1],
        device_id=(tile, lax.rem(rad + n_rad - 1, n_rad)), device_id_type=MESH,
    )
    op_copies = [
        pltpu.make_async_remote_copy(
            src_ref=opsum, dst_ref=oprecv.at[d - 1],
            send_sem=op_send.at[d - 1], recv_sem=op_recv.at[d - 1],
            device_id=(tile, lax.rem(rad + d, n_rad)), device_id_type=MESH,
        )
        for d in range(1, n_rad)
    ]

    def await_signals(semaphore, amount):
        @pl.when(amount > 0)
        def _():
            pl.semaphore_wait(semaphore, amount)

    await_signals(barrier, tile + rad)

    def report_tile(d):
        @pl.when(tile >= d)
        def _():
            other = tile - d

            after = jnp.logical_and(place == 0, d == 1)

            @pl.when(beside(other))
            def _():
                signal(side_sem, other, rad)

            @pl.when(after)
            def _():
                signal(turn_sem, other, rad)

            @pl.when(jnp.logical_not(jnp.logical_or(beside(other), after)))
            def _():
                signal(far_sem, other, rad)

    def report_rad(d):
        @pl.when(rad >= d)
        def _():
            signal(rad_sem, tile, rad - d)

    report_tile(1)
    start_hops(0)
    start_beside(1, order[:EARLY])
    for copy in load_small[:3] + load_x2:
        copy.start()
    start_crossing(whole[:CROSS], 0, nxt < tile)
    start_crossing(whole[:CROSS], 1, prv < tile)
    if n_tile <= 8:
        for d in range(n_tile - 1, 1, -1):
            report_tile(d)
    else:
        lax.fori_loop(2, n_tile, lambda d, c: (report_tile(d), c)[1], 0)
    each(n_rad, report_rad)

    @pl.when(has_below)
    def _():
        lvl_down.start()

    for copy in load_small[3:]:
        copy.start()
    load_ext.start()
    for copy in load_small[:3]:
        copy.wait()

    def fill_taps(span):
        diff = lax.broadcasted_iota(jnp.int32, (C, T), 0) - dcol[...]
        rows = drow[...]
        for r in span:
            weights = []
            for b in range(4):
                w = jnp.zeros((1, T), jnp.float32)
                for a in range(4):
                    w = jnp.where(rows + a == r, lagrange[4 * a + b : 4 * a + b + 1, :], w)
                weights.append(w)
            g = jnp.where(diff == 0, weights[0], 0.0)
            for b in range(1, 4):
                g = jnp.where(diff == b, weights[b], g)
            taps[0, r], taps[1, r] = split(g)

    fill_taps(range(HEAD))
    await_signals(side_sem, side_higher)
    start_hops(1)
    start_beside(0, order[:EARLY])
    fill_taps(range(HEAD, R))
    await_signals(turn_sem, turn_higher)
    start_crossing(whole[:CROSS_UP], 0, nxt > tile)
    await_signals(rad_sem, n_rad - 1 - rad)

    @pl.when(has_above)
    def _():
        lvl_up.start()

    for copy in load_x2:
        copy.wait()
    values = jnp.zeros((V, T), jnp.float32)
    for r in range(R):
        gh = taps[0, r]
        gl = taps[1, r]
        xh, xl = split(
            jnp.concatenate([x2[h, pl.ds(r, V, stride=R), :] for h in range(halves)], axis=1)
        )
        values = values + (dot(xh, gh) + (dot(xl, gh) + dot(xh, gl)))

    for copy in load_small[3:]:
        copy.wait()
    target = ttile[...]
    kinds = max(16, n_tile)
    hot = (lax.broadcasted_iota(jnp.int32, (kinds, T), 0) == target).astype(jnp.float32)
    before = (
        lax.broadcasted_iota(jnp.int32, (T, T), 0) < lax.broadcasted_iota(jnp.int32, (T, T), 1)
    ).astype(jnp.float32)
    earlier = dot(hot.astype(jnp.bfloat16), before.astype(jnp.bfloat16))
    rank = jnp.sum(earlier * hot, axis=0, keepdims=True)
    key = target * cap + rank.astype(jnp.int32)
    lane_slot = lax.rem(lax.broadcasted_iota(jnp.int32, (LANES, T), 0), cap)
    vh, vl = split(values)
    label = tcell[...]
    side = lax.broadcasted_iota(jnp.int32, (16, T), 0)
    label = jnp.where(
        side == 0, label // C + 1, jnp.where(side == 1, lax.rem(label, C), 0)
    ).astype(jnp.float32).astype(jnp.bfloat16)
    stacked = jnp.concatenate([vh, vl, label], axis=0)
    lane_group = lax.broadcasted_iota(jnp.int32, (VP, LANES), 1) // cap

    def chunk(d):
        first = lax.rem(tile + d, n_tile) * cap
        chosen = (key == lane_slot + first).astype(jnp.float32).astype(jnp.bfloat16)
        moved = lax.dot_general(stacked, chosen, NT, preferred_element_type=jnp.float32)
        full = moved[:V] + moved[V : 2 * V]
        picked = full[:VP]
        for g in range(1, pack):
            picked = jnp.where(lane_group == g, full[g * VP : (g + 1) * VP], picked)
        return picked, moved[2 * V : 2 * V + 8]

    await_signals(far_sem, n_tile - 1 - tile - side_higher - turn_higher)
    start_crossing(whole[:CROSS], 1, prv > tile)
    if relays:
        for f in relayed[:SOON]:
            forward(f)

    used = pl.ds(0, VP + 2)

    def a2a_copy(d):
        return pltpu.make_async_remote_copy(
            src_ref=chunks.at[d, used], dst_ref=inc.at[d, used],
            send_sem=a2a_send, recv_sem=a2a_recv.at[d],
            device_id=(lax.rem(tile + d, n_tile), rad), device_id_type=MESH,
        )

    def fill_chunk(d):
        picked, marks = chunk(d)
        chunks[d, pl.ds(0, VP)] = picked
        chunks[d, pl.ds(VP, 8)] = marks

    if n_tile <= 8:
        turns = sorted(range(1, n_tile), key=lambda d: abs(2 * d - n_tile))
        for k, d in enumerate(turns):
            fill_chunk(d)
            if k:
                a2a_copy(turns[k - 1]).start()
        a2a_copy(turns[-1]).start()
    else:
        each(n_tile, fill_chunk)
        each(n_tile, lambda d: a2a_copy(d).start())
    opsum[...] = jnp.sum(opacity[...], axis=0)
    start_crossing(whole[CROSS_UP:], 0, nxt > tile)
    start_crossing(whole[CROSS:], 0, nxt < tile)
    start_crossing(whole[CROSS:], 1, tile >= 0)
    start_beside(1, order[EARLY:])
    start_beside(0, order[EARLY:])
    picked, marks = chunk(0)
    inc[0, pl.ds(0, VP)] = picked
    inc[0, pl.ds(VP, 8)] = marks
    for copy in op_copies:
        copy.start()

    load_ext.wait()
    zeros3 = jnp.zeros((F, 3, R, C), jnp.float32)

    @pl.when(has_below)
    def _():
        lvl_up.wait_recv()

    @pl.when(jnp.logical_not(has_below))
    def _():
        ext[:, pl.ds(0, 3)] = zeros3

    @pl.when(has_above)
    def _():
        lvl_down.wait_recv()

    @pl.when(jnp.logical_not(has_above))
    def _():
        ext[:, pl.ds(L + 3, 3)] = zeros3

    no_rows = jnp.zeros((F, L, 3, C), jnp.float32)

    @pl.when(jnp.logical_not(has_prev))
    def _():
        edge[:, :, strip[0]] = no_rows

    @pl.when(jnp.logical_not(has_next))
    def _():
        edge[:, :, strip[1]] = no_rows

    column = lax.broadcasted_iota(jnp.int32, (STEP, R, C), 2)

    def local_part(f, i, carry):
        l = i * STEP
        u = ext[f, pl.ds(l + 3, STEP)]
        speed1 = ext[1, pl.ds(l + 3, STEP)]
        speed3 = ext[3, pl.ds(l + 3, STEP)]
        ups = [ext[f, pl.ds(l + 3 + k, STEP)] for k in (1, 2, 3)]
        downs = [ext[f, pl.ds(l + 3 - k, STEP)] for k in (1, 2, 3)]
        first, second = pair_terms(u, ups, downs)
        total = VISCOSITY * second - speed1 * first
        ups = [jnp.where(column < C - k, pltpu.roll(u, C - k, 2), 0.0) for k in (1, 2, 3)]
        downs = [jnp.where(column >= k, pltpu.roll(u, k, 2), 0.0) for k in (1, 2, 3)]
        first, second = pair_terms(u, ups, downs)
        acc[f, pl.ds(l, STEP)] = total + (VISCOSITY * second - speed3 * first)
        return carry

    for f in range(F):
        lax.fori_loop(0, L // STEP, functools.partial(local_part, f), 0)
        if f >= FIRST:
            for g in relayed[SOON + f - FIRST : SOON + f - FIRST + 1]:
                forward(g)

    above = jnp.zeros((R, C), jnp.float32)
    for d in range(1, n_rad):
        op_copies[d - 1].wait_recv()
        above = above + jnp.where(rad >= d, oprecv[d - 1], 0.0)

    def cool(l, so_far):
        mine = opacity[l]
        depth = so_far + 0.5 * mine
        acc[7, l] = acc[7, l] - COOL_RATE * jnp.exp(-depth) * ext[7, l + 3]
        return so_far + mine

    lax.fori_loop(0, L, cool, above)

    row = lax.broadcasted_iota(jnp.int32, (STEP, R, C), 1)

    def await_rows(f):
        @pl.when(has_prev)
        def _():
            row_copy(f, 0).wait_recv()

        @pl.when(has_next)
        def _():
            row_copy(f, 1).wait_recv()

    def received(f, l):
        at = pl.ds(pl.multiple_of((f * L + l) * R, STEP * R), STEP * R)
        return jnp.concatenate(
            [ghost[h, at, :].reshape(STEP, R, LANES) for h in range(halves)], axis=2
        )

    def row_part(f, keep, i, carry):
        l = i * STEP
        u = ext[f, pl.ds(l + 3, STEP)]
        speed2 = ext[2, pl.ds(l + 3, STEP)]
        rim = edge[f, pl.ds(l, STEP)]
        ups = [pltpu.roll(jnp.where(row < k, rim, u), R - k, 1) for k in (1, 2, 3)]
        downs = [pltpu.roll(jnp.where(row >= R - k, rim, u), k, 1) for k in (1, 2, 3)]
        if keep is not None:
            sums = [a + b for a, b in zip(ups, downs)]
            jumps = [a - b for a, b in zip(ups, downs)]
            spread = sum(w * a for w, a in zip(SPREAD, sums))
            slope = sum(w * a for w, a in zip(SLOPE, jumps))
            total = TIME_STEP * (acc[f, pl.ds(l, STEP)] + COUPLING * received(f, l))
            total = total + keep * u + (spread - speed2 * slope)
        else:
            first, second = pair_terms(u, ups, downs)
            total = acc[f, pl.ds(l, STEP)] + (VISCOSITY * second - speed2 * first)
        acc[f, pl.ds(l, STEP)] = total
        return carry

    def ghost_part(f, i, carry):
        l = i * STEP
        u = ext[f, pl.ds(l + 3, STEP)]
        total = acc[f, pl.ds(l, STEP)] + COUPLING * (received(f, l) - hits[...] * u)
        acc[f, pl.ds(l, STEP)] = u + TIME_STEP * total
        return carry

    for f in order[:PRE]:
        await_rows(f)
        lax.fori_loop(0, L // STEP, functools.partial(row_part, f, None), 0)

    group_of = lax.broadcasted_iota(jnp.int32, (1, LANES), 1) // cap
    row_marks = {}
    column_marks = {}
    for d0 in sorted(range(0, n_tile, pack), key=lambda d: abs(2 * d + 1 - n_tile)):
        for d in range(max(d0, 1), d0 + pack):
            a2a_copy(d).wait_recv()
        lanes = pl.ds(d0 // pack * LANES, LANES)
        parts = [inc[d0 + j] for j in range(pack)]
        for g in range(pack):
            joined = None
            for j in range(pack):
                part = parts[j][:VP]
                turn = ((j - g) * cap) % LANES
                if turn:
                    part = pltpu.roll(part, turn, 1)
                joined = part if joined is None else jnp.where(lane_group == j, part, joined)
            high, low = split(joined)
            xall[pl.ds(g * VP, VP), lanes] = high
            xall[pl.ds(V + g * VP, VP), lanes] = low
        xall[pl.ds(2 * V, 16), lanes] = jnp.ones((16, LANES), jnp.bfloat16)
        row_mark = parts[0][VP : VP + 1]
        column_mark = parts[0][VP + 1 : VP + 2]
        for j in range(1, pack):
            row_mark = jnp.where(group_of == j, parts[j][VP : VP + 1], row_mark)
            column_mark = jnp.where(group_of == j, parts[j][VP + 1 : VP + 2], column_mark)
        row_marks[d0] = row_mark
        column_marks[d0] = column_mark
    row_mark = jnp.concatenate([row_marks[d] for d in sorted(row_marks)], axis=1).astype(jnp.int32)
    column_mark = jnp.concatenate([column_marks[d] for d in sorted(column_marks)], axis=1).astype(jnp.int32)
    slots = n_tile * cap
    cell_column = lax.broadcasted_iota(jnp.int32, (C, slots), 0)
    everything = xall[...]
    for r in range(R):
        wanted = jnp.where(row_mark == r + 1, column_mark, -1)
        place = (cell_column == wanted).astype(jnp.float32).astype(jnp.bfloat16)
        got = lax.dot_general(everything, place, NT, preferred_element_type=jnp.float32)
        total = got[:V] + got[V : 2 * V]
        for h in range(halves):
            ghost[h, pl.ds(r, V, stride=R), :] = total[:, h * LANES : (h + 1) * LANES]
        hits[pl.ds(r, 1), :] = got[2 * V : 2 * V + 1]


    def drain():
        @pl.when(has_above)
        def _():
            lvl_up.wait_send()

        @pl.when(has_below)
        def _():
            lvl_down.wait_send()

        for copy in op_copies:
            copy.wait_send()
        for f in relayed:
            for way in range(2):
                @pl.when(jnp.logical_and(forwards[way], by_relay(f, way, origin[way])))
                def _():
                    forward_copy(f, way).wait_send()

    def drain_rest():
        pltpu.make_async_remote_copy(
            src_ref=chunks.at[pl.ds(1, n_tile - 1), used],
            dst_ref=inc.at[pl.ds(1, n_tile - 1), used],
            send_sem=a2a_send, recv_sem=a2a_recv.at[1],
            device_id=(nxt, rad), device_id_type=MESH,
        ).wait_send()
        for way in range(2):
            @pl.when(sends[way])
            def _():
                pltpu.make_async_remote_copy(
                    src_ref=f4.at[:, :, strip[way]], dst_ref=edge.at[:, :, strip[way]],
                    send_sem=row_send.at[way], recv_sem=row_recv.at[0, way],
                    device_id=(partner[way], rad), device_id_type=MESH,
                ).wait_send()

    for f in order[:PRE]:
        lax.fori_loop(0, L // STEP, functools.partial(ghost_part, f), 0)
    keep = (1.0 + TIME_STEP * VISCOSITY * (-490.0 / 180.0)) - TIME_STEP * COUPLING * hits[...]
    for f in order[PRE:]:
        if f == order[-1]:
            drain()
        await_rows(f)
        lax.fori_loop(0, L // STEP, functools.partial(row_part, f, keep), 0)

    drain_rest()


def shards(n_tile, n_rad, inner, fields, opacity, donor_row, donor_column, target_tile, target_cell, lagrange):
    F, L, R, C = fields.shape
    V = F * L
    T = donor_row.shape[0]
    cap = max(16, 2 * T // n_tile)
    pack = LANES // cap
    VP = V // pack
    hbm = pl.BlockSpec(memory_space=pltpu.HBM)
    vmem = pl.BlockSpec(memory_space=pltpu.VMEM)
    dma = pltpu.SemaphoreType.DMA
    f32 = jnp.float32
    return pl.pallas_call(
        functools.partial(kernel, n_tile, n_rad, inner, cap),
        out_shape=pltpu.VMEM(fields.shape, f32),
        in_specs=[hbm] * 8,
        out_specs=vmem,
        scratch_shapes=[
            pltpu.VMEM((C // LANES, V * R, LANES), f32),
            pltpu.VMEM((F, L + 6, R, C), f32),
            pltpu.VMEM((2, R, C, T), jnp.bfloat16),
            pltpu.VMEM((F, L, R, C), f32),
            pltpu.VMEM((F - F // 2 + 1, L, R, C), f32),
            pltpu.VMEM((C // LANES, V * R, LANES), f32),
            pltpu.VMEM((R, C), f32),
            pltpu.VMEM((n_tile, VP + 8, LANES), f32),
            pltpu.VMEM((n_tile, VP + 8, LANES), f32),
            pltpu.VMEM((2 * V + 16, n_tile * cap), jnp.bfloat16),
            pltpu.VMEM((R, C), f32),
            pltpu.VMEM((n_rad - 1, R, C), f32),
            pltpu.VMEM((L, R, C), f32),
            pltpu.VMEM((1, T), jnp.int32),
            pltpu.VMEM((1, T), jnp.int32),
            pltpu.VMEM((1, T), jnp.int32),
            pltpu.VMEM((1, T), jnp.int32),
            pltpu.VMEM(lagrange.shape, f32),
            dma((C // LANES,)),
            dma(()),
            dma((6,)),
            pltpu.SemaphoreType.REGULAR,
            pltpu.SemaphoreType.REGULAR,
            pltpu.SemaphoreType.REGULAR,
            pltpu.SemaphoreType.REGULAR,
            dma((2,)),
            dma((2,)),
            dma((2,)),
            dma((F, 2)),
            dma((F - F // 2 + 1, 2)),
            dma((F - F // 2 + 1, 2)),
            dma((n_rad - 1,)),
            dma((n_rad - 1,)),
            dma(()),
            dma((n_tile,)),
        ],
        compiler_params=pltpu.CompilerParams(
            collective_id=0, has_side_effects=True, vmem_limit_bytes=VMEM_LIMIT
        ),
    )(
        in_hbm(fields),
        in_hbm(fields.reshape(V * R, C)),
        in_hbm(opacity),
        in_hbm(donor_row.reshape(1, T)),
        in_hbm(donor_column.reshape(1, T)),
        in_hbm(target_tile.reshape(1, T)),
        in_hbm(target_cell.reshape(1, T)),
        in_hbm(lagrange),
    )


def line_length(mesh):
    devices = mesh.devices[:, 0]
    spots = [getattr(device, "coords", None) for device in devices]
    if spots[0] is None:
        return len(spots)
    moved = [k for k in range(3) if len(spots) > 1 and spots[1][k] != spots[0][k]]
    if len(moved) != 1:
        return len(spots)
    count = 1
    while count < len(spots) and all(
        spots[count][k] == spots[0][k] for k in range(3) if k != moved[0]
    ):
        count += 1
    return count


def solution(mesh):
    in_specs = (
        P(None, "rad", "tile", None),
        P("rad", "tile", None),
        P("tile"),
        P("tile"),
        P("tile", None),
        P("tile"),
        P(None, "tile"),
    )
    out_specs = P(None, "rad", "tile", None)
    body = functools.partial(shards, mesh.shape["tile"], mesh.shape["rad"], line_length(mesh))
    return jax.shard_map(body, mesh=mesh, in_specs=in_specs, out_specs=out_specs, check_vma=False)
```

```python
import functools

import jax
import jax.numpy as jnp
from jax import lax
from jax.experimental import pallas as pl
from jax.experimental.pallas import tpu as pltpu
from jax.sharding import PartitionSpec as P

VISCOSITY = 0.1
COUPLING = 1.0
COOL_RATE = 2.0
TIME_STEP = 0.2
MESH = pl.DeviceIdType.MESH
LANES = 128
EVEN = lambda r: lax.rem(r, 2) == 0
NONE = lambda r: r < 0
VMEM_LIMIT = 32 << 20
STEP = 8
EARLY = 4
CROSS = 2
PRE = 4
HEAD = 1
CROSS_UP = 2
MORE = (EVEN, NONE)
FEWER = (NONE, NONE)
SOON = 2
ORDER = (0, 1, 4, 5, 6, 2, 3, 7)
FIRST = 0
NT = (((1,), (1,)), ((), ()))
SPREAD = [TIME_STEP * VISCOSITY * w / 180.0 for w in (270.0, -27.0, 2.0)]
SLOPE = [TIME_STEP * w / 60.0 for w in (45.0, -9.0, 1.0)]


def in_hbm(x):
    return pltpu.with_memory_space_constraint(x, pltpu.HBM)


def dot(a, b):
    return jnp.dot(a, b, preferred_element_type=jnp.float32)


def split(x):
    high = x.astype(jnp.bfloat16)
    low = (x - high.astype(jnp.float32)).astype(jnp.bfloat16)
    return high, low


def pair_terms(u, ups, downs):
    s1, s2, s3 = [a + b for a, b in zip(ups, downs)]
    d1, d2, d3 = [a - b for a, b in zip(ups, downs)]
    first = (45.0 / 60.0) * d1 - (9.0 / 60.0) * d2 + (1.0 / 60.0) * d3
    second = (
        (270.0 / 180.0) * s1 - (27.0 / 180.0) * s2 + (2.0 / 180.0) * s3 - (490.0 / 180.0) * u
    )
    return first, second


def kernel(
    n_tile, n_rad, inner, cap,
    f4, f2, opacity_in, drow_in, dcol_in, ttile_in, tcell_in, lagrange_in,
    acc,
    x2, ext, taps, edge, relay, ghost, hits, chunks, inc, xall, opsum, oprecv,
    opacity, drow, dcol, ttile, tcell, lagrange,
    x2_sem, in_sem, small_sem, side_sem, turn_sem, rad_sem, far_sem, lvl_send, lvl_recv, row_send, row_recv, hop_recv, fwd_send,
    op_send, op_recv, a2a_send, a2a_recv,
):
    F, L, R, C = acc.shape
    V = F * L
    T = drow.shape[1]
    pack = LANES // cap
    VP = V // pack
    tile = lax.axis_index("tile")
    rad = lax.axis_index("rad")
    quarter = n_tile // 4
    place = lax.rem(tile, inner)
    line = tile // inner

    def each(count, visit):
        if count <= 8:
            for d in range(1, count):
                visit(d)
        else:
            lax.fori_loop(1, count, lambda d, c: (visit(d), c)[1], 0)

    halves = C // LANES
    load_x2 = [
        pltpu.make_async_copy(f2.at[:, pl.ds(h * LANES, LANES)], x2.at[h], x2_sem.at[h])
        for h in range(halves)
    ]
    load_small = [
        pltpu.make_async_copy(source, kept, small_sem.at[k])
        for k, (source, kept) in enumerate(
            [
                (dcol_in, dcol), (drow_in, drow), (lagrange_in, lagrange), (ttile_in, ttile),
                (tcell_in, tcell), (opacity_in, opacity),
            ]
        )
    ]
    load_ext = pltpu.make_async_copy(f4, ext.at[:, pl.ds(3, L)], in_sem)
    def beside(other):
        across = jnp.abs(lax.rem(other, inner) - place)
        return jnp.logical_and(
            other // inner == line, jnp.logical_or(across == 1, across == inner - 1)
        )

    def count(flag):
        return flag.astype(jnp.int32)

    side_higher = count(place < inner - 1)
    turn_higher = count(jnp.logical_and(place == inner - 1, tile < n_tile - 1))
    if inner > 2:
        side_higher = side_higher + count(place == 0)

    def signal(semaphore, to_tile, to_rad):
        pl.semaphore_signal(semaphore, inc=1, device_id=(to_tile, to_rad), device_id_type=MESH)

    barrier = pltpu.get_barrier_semaphore()

    def announce_tile(d):
        @pl.when(tile + d < n_tile)
        def _():
            signal(barrier, tile + d, rad)

    def announce_rad(d):
        @pl.when(rad + d < n_rad)
        def _():
            signal(barrier, tile, rad + d)

    each(n_tile, announce_tile)
    each(n_rad, announce_rad)


    nxt = lax.rem(tile + 1, n_tile)
    prv = lax.rem(tile + n_tile - 1, n_tile)
    has_next = jnp.logical_and(tile != quarter - 1, tile != 3 * quarter - 1)
    has_prev = jnp.logical_and(tile != quarter, tile != 3 * quarter)
    has_above = rad != n_rad - 1
    has_below = rad != 0

    half = F // 2
    relays = inner < n_tile
    order = [f for f in ORDER if f < F] if F == len(ORDER) else list(range(F))
    whole = [f for f in order if f < half or f == F - 1 or not relays]
    crosses = (place == inner - 1, place == 0)
    partner = (nxt, prv)
    via = (tile - (inner - 1), tile + (inner - 1))
    sends = (has_next, has_prev)
    origin = (lax.rem(tile + inner - 1, n_tile), lax.rem(tile + n_tile - inner + 1, n_tile))
    forwards = (
        jnp.logical_and(
            crosses[1],
            jnp.logical_and(origin[0] != quarter - 1, origin[0] != 3 * quarter - 1),
        ),
        jnp.logical_and(
            crosses[0], jnp.logical_and(origin[1] != quarter, origin[1] != 3 * quarter)
        ),
    )
    goal = (lax.rem(origin[0] + 1, n_tile), lax.rem(origin[1] + n_tile - 1, n_tile))
    strip = (pl.ds(R - 3, 3), pl.ds(0, 3))

    def row_copy(f, way):
        return pltpu.make_async_remote_copy(
            src_ref=f4.at[f, :, strip[way]], dst_ref=edge.at[f, :, strip[way]],
            send_sem=row_send.at[way], recv_sem=row_recv.at[f, way],
            device_id=(partner[way], rad), device_id_type=MESH,
        )

    def hop_copy(f, way):
        return pltpu.make_async_remote_copy(
            src_ref=f4.at[f, :, strip[way]], dst_ref=relay.at[f - shared, :, strip[way]],
            send_sem=row_send.at[way], recv_sem=hop_recv.at[f - shared, way],
            device_id=(via[way], rad), device_id_type=MESH,
        )

    def forward_copy(f, way):
        return pltpu.make_async_remote_copy(
            src_ref=relay.at[f - shared, :, strip[way]], dst_ref=edge.at[f, :, strip[way]],
            send_sem=fwd_send.at[f - shared, way], recv_sem=row_recv.at[f, way],
            device_id=(goal[way], rad), device_id_type=MESH,
        )

    shared = half - 1
    relayed = [*range(half, F), shared] if relays else []
    def by_relay(f, way, source):
        wraps = source == (n_tile - 1, 0)[way]
        if f == shared and relays:
            return jnp.logical_and(wraps, MORE[way](rad))
        if f == F - 1 and relays:
            lighter = wraps if way else jnp.logical_not(wraps)
            return jnp.logical_not(jnp.logical_and(lighter, FEWER[way](rad)))
        return jnp.logical_and(tile >= 0, f in relayed and f != shared)

    def start_hops(way):
        for f in relayed:
            through = by_relay(f, way, tile)

            @pl.when(jnp.logical_and(jnp.logical_and(sends[way], crosses[way]), through))
            def _():
                hop_copy(f, way).start()

    def start_beside(way, fields):
        for f in fields:
            @pl.when(jnp.logical_and(sends[way], jnp.logical_not(crosses[way])))
            def _():
                row_copy(f, way).start()

    def start_crossing(fields, way, ready):
        for f in fields:
            direct = jnp.logical_and(ready, jnp.logical_not(by_relay(f, way, tile)))

            @pl.when(jnp.logical_and(jnp.logical_and(sends[way], crosses[way]), direct))
            def _():
                row_copy(f, way).start()

    def forward(f):
        for way in range(2):
            @pl.when(jnp.logical_and(forwards[way], by_relay(f, way, origin[way])))
            def _():
                hop_copy(f, way).wait_recv()
                forward_copy(f, way).start()

    lvl_up = pltpu.make_async_remote_copy(
        src_ref=f4.at[:, pl.ds(L - 3, 3)], dst_ref=ext.at[:, pl.ds(0, 3)],
        send_sem=lvl_send.at[0], recv_sem=lvl_recv.at[0],
        device_id=(tile, lax.rem(rad + 1, n_rad)), device_id_type=MESH,
    )
    lvl_down = pltpu.make_async_remote_copy(
        src_ref=f4.at[:, pl.ds(0, 3)], dst_ref=ext.at[:, pl.ds(L + 3, 3)],
        send_sem=lvl_send.at[1], recv_sem=lvl_recv.at[1],
        device_id=(tile, lax.rem(rad + n_rad - 1, n_rad)), device_id_type=MESH,
    )
    op_copies = [
        pltpu.make_async_remote_copy(
            src_ref=opsum, dst_ref=oprecv.at[d - 1],
            send_sem=op_send.at[d - 1], recv_sem=op_recv.at[d - 1],
            device_id=(tile, lax.rem(rad + d, n_rad)), device_id_type=MESH,
        )
        for d in range(1, n_rad)
    ]

    def await_signals(semaphore, amount):
        @pl.when(amount > 0)
        def _():
            pl.semaphore_wait(semaphore, amount)

    await_signals(barrier, tile + rad)

    def report_tile(d):
        @pl.when(tile >= d)
        def _():
            other = tile - d

            after = jnp.logical_and(place == 0, d == 1)

            @pl.when(beside(other))
            def _():
                signal(side_sem, other, rad)

            @pl.when(after)
            def _():
                signal(turn_sem, other, rad)

            @pl.when(jnp.logical_not(jnp.logical_or(beside(other), after)))
            def _():
                signal(far_sem, other, rad)

    def report_rad(d):
        @pl.when(rad >= d)
        def _():
            signal(rad_sem, tile, rad - d)

    report_tile(1)
    start_hops(0)
    start_beside(1, order[:EARLY])
    for copy in load_small[:3] + load_x2:
        copy.start()
    start_crossing(whole[:CROSS], 0, nxt < tile)
    start_crossing(whole[:CROSS], 1, prv < tile)
    if n_tile <= 8:
        for d in range(n_tile - 1, 1, -1):
            report_tile(d)
    else:
        lax.fori_loop(2, n_tile, lambda d, c: (report_tile(d), c)[1], 0)
    each(n_rad, report_rad)

    @pl.when(has_below)
    def _():
        lvl_down.start()

    for copy in load_small[3:]:
        copy.start()
    load_ext.start()
    for copy in load_small[:3]:
        copy.wait()

    def fill_taps(span):
        diff = lax.broadcasted_iota(jnp.int32, (C, T), 0) - dcol[...]
        rows = drow[...]
        for r in span:
            weights = []
            for b in range(4):
                w = jnp.zeros((1, T), jnp.float32)
                for a in range(4):
                    w = jnp.where(rows + a == r, lagrange[4 * a + b : 4 * a + b + 1, :], w)
                weights.append(w)
            g = jnp.where(diff == 0, weights[0], 0.0)
            for b in range(1, 4):
                g = jnp.where(diff == b, weights[b], g)
            taps[0, r], taps[1, r] = split(g)

    fill_taps(range(HEAD))
    await_signals(side_sem, side_higher)
    start_hops(1)
    start_beside(0, order[:EARLY])
    fill_taps(range(HEAD, R))
    await_signals(turn_sem, turn_higher)
    start_crossing(whole[:CROSS_UP], 0, nxt > tile)
    await_signals(rad_sem, n_rad - 1 - rad)

    @pl.when(has_above)
    def _():
        lvl_up.start()

    for copy in load_x2:
        copy.wait()
    values = jnp.zeros((V, T), jnp.float32)
    for r in range(R):
        gh = taps[0, r]
        gl = taps[1, r]
        xh, xl = split(
            jnp.concatenate([x2[h, pl.ds(r, V, stride=R), :] for h in range(halves)], axis=1)
        )
        values = values + (dot(xh, gh) + (dot(xl, gh) + dot(xh, gl)))

    for copy in load_small[3:]:
        copy.wait()
    target = ttile[...]
    kinds = max(16, n_tile)
    hot = (lax.broadcasted_iota(jnp.int32, (kinds, T), 0) == target).astype(jnp.float32)
    before = (
        lax.broadcasted_iota(jnp.int32, (T, T), 0) < lax.broadcasted_iota(jnp.int32, (T, T), 1)
    ).astype(jnp.float32)
    earlier = dot(hot.astype(jnp.bfloat16), before.astype(jnp.bfloat16))
    rank = jnp.sum(earlier * hot, axis=0, keepdims=True)
    key = target * cap + rank.astype(jnp.int32)
    lane_slot = lax.rem(lax.broadcasted_iota(jnp.int32, (LANES, T), 0), cap)
    vh, vl = split(values)
    label = tcell[...]
    side = lax.broadcasted_iota(jnp.int32, (16, T), 0)
    label = jnp.where(
        side == 0, label // C + 1, jnp.where(side == 1, lax.rem(label, C), 0)
    ).astype(jnp.float32).astype(jnp.bfloat16)
    stacked = jnp.concatenate([vh, vl, label], axis=0)
    lane_group = lax.broadcasted_iota(jnp.int32, (VP, LANES), 1) // cap

    def chunk(d):
        first = lax.rem(tile + d, n_tile) * cap
        chosen = (key == lane_slot + first).astype(jnp.float32).astype(jnp.bfloat16)
        moved = lax.dot_general(stacked, chosen, NT, preferred_element_type=jnp.float32)
        full = moved[:V] + moved[V : 2 * V]
        picked = full[:VP]
        for g in range(1, pack):
            picked = jnp.where(lane_group == g, full[g * VP : (g + 1) * VP], picked)
        return picked, moved[2 * V : 2 * V + 8]

    await_signals(far_sem, n_tile - 1 - tile - side_higher - turn_higher)
    start_crossing(whole[:CROSS], 1, prv > tile)
    if relays:
        for f in relayed[:SOON]:
            forward(f)

    used = pl.ds(0, VP + 2)

    def a2a_copy(d):
        return pltpu.make_async_remote_copy(
            src_ref=chunks.at[d, used], dst_ref=inc.at[d, used],
            send_sem=a2a_send, recv_sem=a2a_recv.at[d],
            device_id=(lax.rem(tile + d, n_tile), rad), device_id_type=MESH,
        )

    def fill_chunk(d):
        picked, marks = chunk(d)
        chunks[d, pl.ds(0, VP)] = picked
        chunks[d, pl.ds(VP, 8)] = marks

    if n_tile <= 8:
        turns = sorted(range(1, n_tile), key=lambda d: abs(2 * d - n_tile))
        for k, d in enumerate(turns):
            fill_chunk(d)
            if k:
                a2a_copy(turns[k - 1]).start()
        a2a_copy(turns[-1]).start()
    else:
        each(n_tile, fill_chunk)
        each(n_tile, lambda d: a2a_copy(d).start())
    opsum[...] = jnp.sum(opacity[...], axis=0)
    start_crossing(whole[CROSS_UP:], 0, nxt > tile)
    start_crossing(whole[CROSS:], 0, nxt < tile)
    start_crossing(whole[CROSS:], 1, tile >= 0)
    start_beside(1, order[EARLY:])
    start_beside(0, order[EARLY:])
    picked, marks = chunk(0)
    inc[0, pl.ds(0, VP)] = picked
    inc[0, pl.ds(VP, 8)] = marks
    for copy in op_copies:
        copy.start()

    load_ext.wait()
    zeros3 = jnp.zeros((F, 3, R, C), jnp.float32)

    @pl.when(has_below)
    def _():
        lvl_up.wait_recv()

    @pl.when(jnp.logical_not(has_below))
    def _():
        ext[:, pl.ds(0, 3)] = zeros3

    @pl.when(has_above)
    def _():
        lvl_down.wait_recv()

    @pl.when(jnp.logical_not(has_above))
    def _():
        ext[:, pl.ds(L + 3, 3)] = zeros3

    no_rows = jnp.zeros((F, L, 3, C), jnp.float32)

    @pl.when(jnp.logical_not(has_prev))
    def _():
        edge[:, :, strip[0]] = no_rows

    @pl.when(jnp.logical_not(has_next))
    def _():
        edge[:, :, strip[1]] = no_rows

    column = lax.broadcasted_iota(jnp.int32, (STEP, R, C), 2)

    def local_part(f, i, carry):
        l = i * STEP
        u = ext[f, pl.ds(l + 3, STEP)]
        speed1 = ext[1, pl.ds(l + 3, STEP)]
        speed3 = ext[3, pl.ds(l + 3, STEP)]
        ups = [ext[f, pl.ds(l + 3 + k, STEP)] for k in (1, 2, 3)]
        downs = [ext[f, pl.ds(l + 3 - k, STEP)] for k in (1, 2, 3)]
        first, second = pair_terms(u, ups, downs)
        total = VISCOSITY * second - speed1 * first
        ups = [jnp.where(column < C - k, pltpu.roll(u, C - k, 2), 0.0) for k in (1, 2, 3)]
        downs = [jnp.where(column >= k, pltpu.roll(u, k, 2), 0.0) for k in (1, 2, 3)]
        first, second = pair_terms(u, ups, downs)
        acc[f, pl.ds(l, STEP)] = total + (VISCOSITY * second - speed3 * first)
        return carry

    for f in range(F):
        lax.fori_loop(0, L // STEP, functools.partial(local_part, f), 0)
        if f >= FIRST:
            for g in relayed[SOON + f - FIRST : SOON + f - FIRST + 1]:
                forward(g)

    above = jnp.zeros((R, C), jnp.float32)
    for d in range(1, n_rad):
        op_copies[d - 1].wait_recv()
        above = above + jnp.where(rad >= d, oprecv[d - 1], 0.0)

    def cool(l, so_far):
        mine = opacity[l]
        depth = so_far + 0.5 * mine
        acc[7, l] = acc[7, l] - COOL_RATE * jnp.exp(-depth) * ext[7, l + 3]
        return so_far + mine

    lax.fori_loop(0, L, cool, above)

    row = lax.broadcasted_iota(jnp.int32, (STEP, R, C), 1)

    def await_rows(f):
        @pl.when(has_prev)
        def _():
            row_copy(f, 0).wait_recv()

        @pl.when(has_next)
        def _():
            row_copy(f, 1).wait_recv()

    def received(f, l):
        at = pl.ds(pl.multiple_of((f * L + l) * R, STEP * R), STEP * R)
        return jnp.concatenate(
            [ghost[h, at, :].reshape(STEP, R, LANES) for h in range(halves)], axis=2
        )

    def row_part(f, keep, i, carry):
        l = i * STEP
        u = ext[f, pl.ds(l + 3, STEP)]
        speed2 = ext[2, pl.ds(l + 3, STEP)]
        rim = edge[f, pl.ds(l, STEP)]
        ups = [pltpu.roll(jnp.where(row < k, rim, u), R - k, 1) for k in (1, 2, 3)]
        downs = [pltpu.roll(jnp.where(row >= R - k, rim, u), k, 1) for k in (1, 2, 3)]
        if keep is not None:
            sums = [a + b for a, b in zip(ups, downs)]
            jumps = [a - b for a, b in zip(ups, downs)]
            spread = sum(w * a for w, a in zip(SPREAD, sums))
            slope = sum(w * a for w, a in zip(SLOPE, jumps))
            total = TIME_STEP * (acc[f, pl.ds(l, STEP)] + COUPLING * received(f, l))
            total = total + keep * u + (spread - speed2 * slope)
        else:
            first, second = pair_terms(u, ups, downs)
            total = acc[f, pl.ds(l, STEP)] + (VISCOSITY * second - speed2 * first)
        acc[f, pl.ds(l, STEP)] = total
        return carry

    def ghost_part(f, i, carry):
        l = i * STEP
        u = ext[f, pl.ds(l + 3, STEP)]
        total = acc[f, pl.ds(l, STEP)] + COUPLING * (received(f, l) - hits[...] * u)
        acc[f, pl.ds(l, STEP)] = u + TIME_STEP * total
        return carry

    for f in order[:PRE]:
        await_rows(f)
        lax.fori_loop(0, L // STEP, functools.partial(row_part, f, None), 0)

    group_of = lax.broadcasted_iota(jnp.int32, (1, LANES), 1) // cap
    row_marks = {}
    column_marks = {}
    for d0 in sorted(range(0, n_tile, pack), key=lambda d: abs(2 * d + 1 - n_tile)):
        for d in range(max(d0, 1), d0 + pack):
            a2a_copy(d).wait_recv()
        lanes = pl.ds(d0 // pack * LANES, LANES)
        parts = [inc[d0 + j] for j in range(pack)]
        for g in range(pack):
            joined = None
            for j in range(pack):
                part = parts[j][:VP]
                turn = ((j - g) * cap) % LANES
                if turn:
                    part = pltpu.roll(part, turn, 1)
                joined = part if joined is None else jnp.where(lane_group == j, part, joined)
            high, low = split(joined)
            xall[pl.ds(g * VP, VP), lanes] = high
            xall[pl.ds(V + g * VP, VP), lanes] = low
        xall[pl.ds(2 * V, 16), lanes] = jnp.ones((16, LANES), jnp.bfloat16)
        row_mark = parts[0][VP : VP + 1]
        column_mark = parts[0][VP + 1 : VP + 2]
        for j in range(1, pack):
            row_mark = jnp.where(group_of == j, parts[j][VP : VP + 1], row_mark)
            column_mark = jnp.where(group_of == j, parts[j][VP + 1 : VP + 2], column_mark)
        row_marks[d0] = row_mark
        column_marks[d0] = column_mark
    row_mark = jnp.concatenate([row_marks[d] for d in sorted(row_marks)], axis=1).astype(jnp.int32)
    column_mark = jnp.concatenate([column_marks[d] for d in sorted(column_marks)], axis=1).astype(jnp.int32)
    slots = n_tile * cap
    cell_column = lax.broadcasted_iota(jnp.int32, (C, slots), 0)
    everything = xall[...]
    for r in range(R):
        wanted = jnp.where(row_mark == r + 1, column_mark, -1)
        place = (cell_column == wanted).astype(jnp.float32).astype(jnp.bfloat16)
        got = lax.dot_general(everything, place, NT, preferred_element_type=jnp.float32)
        total = got[:V] + got[V : 2 * V]
        for h in range(halves):
            ghost[h, pl.ds(r, V, stride=R), :] = total[:, h * LANES : (h + 1) * LANES]
        hits[pl.ds(r, 1), :] = got[2 * V : 2 * V + 1]


    def drain():
        @pl.when(has_above)
        def _():
            lvl_up.wait_send()

        @pl.when(has_below)
        def _():
            lvl_down.wait_send()

        for copy in op_copies:
            copy.wait_send()
        for f in relayed:
            for way in range(2):
                @pl.when(jnp.logical_and(forwards[way], by_relay(f, way, origin[way])))
                def _():
                    forward_copy(f, way).wait_send()

    def drain_rest():
        pltpu.make_async_remote_copy(
            src_ref=chunks.at[pl.ds(1, n_tile - 1), used],
            dst_ref=inc.at[pl.ds(1, n_tile - 1), used],
            send_sem=a2a_send, recv_sem=a2a_recv.at[1],
            device_id=(nxt, rad), device_id_type=MESH,
        ).wait_send()
        for way in range(2):
            @pl.when(sends[way])
            def _():
                pltpu.make_async_remote_copy(
                    src_ref=f4.at[:, :, strip[way]], dst_ref=edge.at[:, :, strip[way]],
                    send_sem=row_send.at[way], recv_sem=row_recv.at[0, way],
                    device_id=(partner[way], rad), device_id_type=MESH,
                ).wait_send()

    for f in order[:PRE]:
        lax.fori_loop(0, L // STEP, functools.partial(ghost_part, f), 0)
    keep = (1.0 + TIME_STEP * VISCOSITY * (-490.0 / 180.0)) - TIME_STEP * COUPLING * hits[...]
    for f in order[PRE:]:
        if f == order[-1]:
            drain()
        await_rows(f)
        lax.fori_loop(0, L // STEP, functools.partial(row_part, f, keep), 0)

    drain_rest()


def shards(n_tile, n_rad, inner, fields, opacity, donor_row, donor_column, target_tile, target_cell, lagrange):
    F, L, R, C = fields.shape
    V = F * L
    T = donor_row.shape[0]
    cap = max(16, 2 * T // n_tile)
    pack = LANES // cap
    VP = V // pack
    hbm = pl.BlockSpec(memory_space=pltpu.HBM)
    vmem = pl.BlockSpec(memory_space=pltpu.VMEM)
    dma = pltpu.SemaphoreType.DMA
    f32 = jnp.float32
    return pl.pallas_call(
        functools.partial(kernel, n_tile, n_rad, inner, cap),
        out_shape=pltpu.VMEM(fields.shape, f32),
        in_specs=[hbm] * 8,
        out_specs=vmem,
        scratch_shapes=[
            pltpu.VMEM((C // LANES, V * R, LANES), f32),
            pltpu.VMEM((F, L + 6, R, C), f32),
            pltpu.VMEM((2, R, C, T), jnp.bfloat16),
            pltpu.VMEM((F, L, R, C), f32),
            pltpu.VMEM((F - F // 2 + 1, L, R, C), f32),
            pltpu.VMEM((C // LANES, V * R, LANES), f32),
            pltpu.VMEM((R, C), f32),
            pltpu.VMEM((n_tile, VP + 8, LANES), f32),
            pltpu.VMEM((n_tile, VP + 8, LANES), f32),
            pltpu.VMEM((2 * V + 16, n_tile * cap), jnp.bfloat16),
            pltpu.VMEM((R, C), f32),
            pltpu.VMEM((n_rad - 1, R, C), f32),
            pltpu.VMEM((L, R, C), f32),
            pltpu.VMEM((1, T), jnp.int32),
            pltpu.VMEM((1, T), jnp.int32),
            pltpu.VMEM((1, T), jnp.int32),
            pltpu.VMEM((1, T), jnp.int32),
            pltpu.VMEM(lagrange.shape, f32),
            dma((C // LANES,)),
            dma(()),
            dma((6,)),
            pltpu.SemaphoreType.REGULAR,
            pltpu.SemaphoreType.REGULAR,
            pltpu.SemaphoreType.REGULAR,
            pltpu.SemaphoreType.REGULAR,
            dma((2,)),
            dma((2,)),
            dma((2,)),
            dma((F, 2)),
            dma((F - F // 2 + 1, 2)),
            dma((F - F // 2 + 1, 2)),
            dma((n_rad - 1,)),
            dma((n_rad - 1,)),
            dma(()),
            dma((n_tile,)),
        ],
        compiler_params=pltpu.CompilerParams(
            collective_id=0, has_side_effects=True, vmem_limit_bytes=VMEM_LIMIT
        ),
    )(
        in_hbm(fields),
        in_hbm(fields.reshape(V * R, C)),
        in_hbm(opacity),
        in_hbm(donor_row.reshape(1, T)),
        in_hbm(donor_column.reshape(1, T)),
        in_hbm(target_tile.reshape(1, T)),
        in_hbm(target_cell.reshape(1, T)),
        in_hbm(lagrange),
    )


def line_length(mesh):
    devices = mesh.devices[:, 0]
    spots = [getattr(device, "coords", None) for device in devices]
    if spots[0] is None:
        return len(spots)
    moved = [k for k in range(3) if len(spots) > 1 and spots[1][k] != spots[0][k]]
    if len(moved) != 1:
        return len(spots)
    count = 1
    while count < len(spots) and all(
        spots[count][k] == spots[0][k] for k in range(3) if k != moved[0]
    ):
        count += 1
    return count


def solution(mesh):
    in_specs = (
        P(None, "rad", "tile", None),
        P("rad", "tile", None),
        P("tile"),
        P("tile"),
        P("tile", None),
        P("tile"),
        P(None, "tile"),
    )
    out_specs = P(None, "rad", "tile", None)
    body = functools.partial(shards, mesh.shape["tile"], mesh.shape["rad"], line_length(mesh))
    return jax.shard_map(body, mesh=mesh, in_specs=in_specs, out_specs=out_specs, check_vma=False)
```
